256 devices in a mesh: sect: 8 (over y, core), dir: 32 (over z, x).
Axes of the slice: x: 4, y: 4, z: 8, core: 2. Of those that a mesh axis runs over, the one named last changes fastest.
Arguments:
- unknowns: bfloat16 [2, 16, 64, 128, 256], P(None, 'sect', 'dir'), may hold values from -6 to 6
- leaf_live: int32 [16, 64], P('sect', 'dir'), may hold values from 0 to 1, as said below
- near_blocks: bfloat16 [2, 16, 64, 9, 128, 128], P(None, 'sect', 'dir'), may hold values from -0.125 to 0.125
- aggregate: bfloat16 [2, 16, 64, 512, 128], P(None, 'sect', 'dir'), may hold values from -0.1875 to 0.1875
- disaggregate: bfloat16 [2, 16, 64, 128, 512], P(None, 'sect', 'dir'), may hold values from -0.1875 to 0.1875
- translate: float32 [16, 2, 512], P(None, None, 'dir'), may hold values from -1.2 to 1.2
Outputs:
- field: float32 [2, 16, 64, 128, 256], P(None, 'sect', 'dir')
The draws below stay inside these ranges and needn't reach their ends.
Inputs may be any that keep to these rules, and one draw needn't show every extreme that they name: `leaf_live`: every 2 x 2 block of leaves (one coarse box) has its first leaf live; in every draw some box has all four leaves live.
All inputs are finite; a program needn't handle non-finite values.
Results may differ from the reference program's by a relative error of at most 0.0036.
Values may be sent and summed in bfloat16 or wider, within the bound.
A program may use at most 64 MiB of HBM per device.

```python
import jax
import jax.numpy as jnp
from jax import lax

LS = 128
Q = 512
R = 256
BROWS = 8
BCOLS = 32
LROWS = 16
LCOLS = 64


def draw_leaf_live(key, part):
    first_key, second_key, third_key = jax.random.split(jax.random.fold_in(key, 7), 3)
    random_live = jax.random.randint(first_key, (LROWS, LCOLS), 0, 2)
    row_index = jnp.arange(LROWS, dtype=jnp.int32)[:, None]
    col_index = jnp.arange(LCOLS, dtype=jnp.int32)[None, :]
    first_leaf = ((row_index % 2 == 0) & (col_index % 2 == 0)).astype(jnp.int32)
    full_row = jax.random.randint(second_key, (), 0, BROWS)
    full_col = jax.random.randint(third_key, (), 0, BCOLS)
    full_box = ((row_index // 2 == full_row) & (col_index // 2 == full_col)).astype(jnp.int32)
    return jnp.maximum(jnp.maximum(random_live, first_leaf), full_box).astype(jnp.int32)


def levels(stream_key, dims, shards, smallest, high):
    level, own = 1.0, jax.random.fold_in(stream_key, 6)
    for position, blocks in shards:
        steps = jnp.exp(jax.random.uniform(jax.random.fold_in(own, position), (blocks,), jnp.float32, smallest / len(shards), high / len(shards)))
        level = level * jnp.repeat(steps, dims[position] // blocks).reshape([-1 if axis == position else 1 for axis in range(len(dims))])
    return level


def gaussian(key, dims, width, bound, pieces=(), kind=jnp.bfloat16):
    array = jax.random.normal(key, dims, jnp.float32) * width
    if len(pieces) > 0:
        array = levels(key, dims, pieces, -0.22, 0.18) * array
    return jnp.clip(array, min=-bound, max=bound).astype(kind)


def setup_inputs(seed: int = 0) -> dict:
    keys = jax.random.split(jax.random.key(seed), 7)
    unknowns = gaussian(keys[0], (2, LROWS, LCOLS, LS, R), 1.0, 6.0, ((1, 8), (2, 32)))
    leaf_live = draw_leaf_live(jax.random.fold_in(keys[6], 71), 0)
    near_blocks = gaussian(keys[2], (2, LROWS, LCOLS, 9, LS, LS), (18 * LS) ** -0.5, 0.125, ((1, 8), (2, 32)))
    aggregate = gaussian(keys[3], (2, LROWS, LCOLS, Q, LS), (8 * LS) ** -0.5, 0.1875, ((1, 8), (2, 32)))
    disaggregate = gaussian(keys[4], (2, LROWS, LCOLS, LS, Q), (2 * Q) ** -0.5, 0.1875, ((1, 8), (2, 32)))
    translate = gaussian(keys[5], (16, 2, Q), 0.2, 1.2, ((2, 32),), jnp.float32)
    return dict(unknowns=unknowns, leaf_live=leaf_live, near_blocks=near_blocks, aggregate=aggregate, disaggregate=disaggregate, translate=translate)


far_offsets = [(row_step, col_step) for row_step in range(-2, 3) for col_step in range(-2, 3) if max(abs(row_step), abs(col_step)) == 2]


def complex_einsum(form, left, right):
    left = left.astype(jnp.float32)
    right = right.astype(jnp.float32)
    real = jnp.einsum(form, left[0], right[0]) - jnp.einsum(form, left[1], right[1])
    imag = jnp.einsum(form, left[0], right[1]) + jnp.einsum(form, left[1], right[0])
    return jnp.stack([real, imag])


def reference(unknowns, leaf_live, near_blocks, aggregate, disaggregate, translate):
    live = leaf_live.astype(jnp.float32)[None, :, :, None, None]
    masked = (unknowns.astype(jnp.float32) * live).astype(jnp.bfloat16)
    padded = jnp.pad(masked, ((0, 0), (1, 1), (1, 1), (0, 0), (0, 0)))
    near = jnp.zeros(unknowns.shape, jnp.float32)
    for row_step in range(-1, 2):
        for col_step in range(-1, 2):
            which = (row_step + 1) * 3 + col_step + 1
            beside = padded[:, 1 + row_step:1 + row_step + LROWS, 1 + col_step:1 + col_step + LCOLS]
            near = near + complex_einsum("ijmn,ijnr->ijmr", near_blocks[:, :, :, which], beside)
    agg_view = aggregate.reshape(2, BROWS, 2, BCOLS, 2, Q, LS)
    leaf_view = masked.reshape(2, BROWS, 2, BCOLS, 2, LS, R)
    patterns = complex_einsum("aubvqn,aubvnr->abqr", agg_view, leaf_view).astype(jnp.bfloat16)
    source = jnp.pad(patterns.astype(jnp.float32), ((0, 0), (0, 0), (2, 2), (0, 0), (0, 0)))
    rows_in = []
    for target in range(BROWS):
        total = jnp.zeros((2, BCOLS, Q, R), jnp.float32)
        for row_step in range(-2, 3):
            anchor = target + row_step
            if 0 <= anchor < BROWS:
                term = jnp.zeros((2, BCOLS, Q, R), jnp.float32)
                for index, (step_row, step_col) in enumerate(far_offsets):
                    if step_row == row_step:
                        shifted = source[:, anchor, 2 + step_col:2 + step_col + BCOLS]
                        coef_real = translate[index, 0][None, :, None]
                        coef_imag = translate[index, 1][None, :, None]
                        real = coef_real * shifted[0] - coef_imag * shifted[1]
                        imag = coef_real * shifted[1] + coef_imag * shifted[0]
                        term = term + jnp.stack([real, imag])
                rounded = lax.optimization_barrier(term.astype(jnp.bfloat16))
                total = total + rounded.astype(jnp.float32)
        rows_in.append(total.astype(jnp.bfloat16))
    incoming = jnp.stack(rows_in, axis=1)
    dis_view = disaggregate.reshape(2, BROWS, 2, BCOLS, 2, LS, Q)
    far = complex_einsum("aubvmq,abqr->aubvmr", dis_view, incoming).reshape(2, LROWS, LCOLS, LS, R)
    return (near + far) * live
```

```python
import functools

import jax
import jax.numpy as jnp
from jax import lax
from jax.experimental import pallas as pl
from jax.experimental.pallas import tpu as pltpu
from jax.sharding import PartitionSpec as P

MESH = pl.DeviceIdType.MESH
PLANE_COLS = 4
LANES = 128

far_offsets = [(a, b) for a in range(-2, 3) for b in range(-2, 3) if max(abs(a), abs(b)) == 2]


def stacked(real, imag, axis=0):
    top = jnp.concatenate([real, imag], axis=1)
    low = jnp.concatenate([-imag, real], axis=1)
    return jnp.concatenate([top, low], axis=0)


def dot(left, right):
    return jnp.dot(left, right, preferred_element_type=jnp.float32)


def kernel(
    ns, nd, live_ref, unk_hbm, nb_hbm, agg_hbm, dis_hbm, tr_ref, out_hbm,
    raw, leaves, nb, agg, dis, pat, grid, inc, back, acc, trs, trd, coef,
    load_sem, nx_sem, ny_sem, t_sem, s1_sem, r1_sem, sz_sem, rz_sem, s2_sem, r2_sem, out_sem,
):
    nx = PLANE_COLS
    nz = nd // nx
    owners = ns * nx
    total_dirs = agg.shape[3]
    nq = total_dirs // owners
    f32, bf16 = jnp.float32, jnp.bfloat16

    s, d = lax.axis_index("sect"), lax.axis_index("dir")
    z, x = d // nx, lax.rem(d, nx)
    me = s * nx + x

    loads = [
        pltpu.make_async_copy(src, dst, load_sem.at[i])
        for i, (src, dst) in enumerate(((unk_hbm, raw), (agg_hbm, agg), (nb_hbm, nb), (dis_hbm, dis)))
    ]
    loads[0].start()
    loads[1].start()

    def owner_device(t):
        return (t // nx, z * nx + lax.rem(t, nx))

    bar = pltpu.get_barrier_semaphore()

    def greet(device):
        pl.semaphore_signal(bar, inc=1, device_id=device, device_id_type=MESH)

    @pl.loop(1, owners)
    def _(i):
        greet(owner_device(lax.rem(me + i, owners)))

    for step in (1, nz - 1):
        greet((s, lax.rem(z + step, nz) * nx + x))
    for step in (1, nd - 1):
        greet((s, lax.rem(d + step, nd)))

    @pl.when(s != z)
    def _():
        greet((z, s * nx + x))

    def clear(ref):
        ref[...] = jnp.zeros(ref.shape, ref.dtype)

    @pl.when(s == 0)
    def _():
        clear(leaves.at[0])

    @pl.when(s == ns - 1)
    def _():
        clear(leaves.at[3])

    @pl.when(d == 0)
    def _():
        clear(leaves.at[1:3, 0])

    @pl.when(d == nd - 1)
    def _():
        clear(leaves.at[1:3, 3])

    for rc in range(2):
        clear(grid.at[rc, 0:2])
        clear(grid.at[rc, ns + 2 : ns + 4])

    @pl.when(z == 0)
    def _():
        for rc in range(2):
            clear(grid.at[rc, 2 : ns + 2, 0:2])

    @pl.when(z == nz - 1)
    def _():
        for rc in range(2):
            clear(grid.at[rc, 2 : ns + 2, nx + 2 : nx + 4])

    clear(trs)
    for k in range(16):
        trs[2 * k : 2 * k + 2, 0:nq] = tr_ref[k]
    loads[0].wait()
    loads[2].start()
    loads[3].start()
    for i in range(2):
        for j in range(2):
            live = live_ref[i, j].astype(f32)
            for c in range(2):
                leaves[1 + i, 1 + j, c] = (raw[c, i, j].astype(f32) * live).astype(bf16)

    pl.semaphore_wait(bar, owners - 1 + 4 + jnp.where(s != z, 1, 0))

    def remote(src, dst, sems, i, device):
        return pltpu.make_async_remote_copy(
            src_ref=src, dst_ref=dst, send_sem=sems.at[0, i], recv_sem=sems.at[1, i],
            device_id=device, device_id_type=MESH,
        )

    swap = remote(trs, trd, t_sem, 0, (z, s * nx + x))

    @pl.when(s != z)
    def _():
        swap.start()

    @pl.when(s == z)
    def _():
        trd[...] = trs[...]

    to_left = remote(leaves.at[1:3, 1], leaves.at[1:3, 3], nx_sem, 0, (s, d - 1))
    to_right = remote(leaves.at[1:3, 2], leaves.at[1:3, 0], nx_sem, 1, (s, d + 1))

    spans = ((1, 3), (0, 1), (3, 4))
    up = [
        remote(leaves.at[1, a:b], leaves.at[3, a:b], ny_sem, i, (s - 1, d)) for i, (a, b) in enumerate(spans)
    ]
    down = [
        remote(leaves.at[2, a:b], leaves.at[0, a:b], ny_sem, 3 + i, (s + 1, d)) for i, (a, b) in enumerate(spans)
    ]

    def start_columns():
        @pl.when(d > 0)
        def _():
            to_left.start()

        @pl.when(d < nd - 1)
        def _():
            to_right.start()

    def start_rows(which):
        @pl.when(s > 0)
        def _():
            for i in which:
                up[i].start()

        @pl.when(s < ns - 1)
        def _():
            for i in which:
                down[i].start()

    def lanes(rc):
        return pl.ds(rc * LANES, LANES)

    def dirs_of(t):
        return pl.ds(pl.multiple_of(t * nq, nq), nq)

    loads[1].wait()
    for rc in range(2):
        cols = slice(rc * LANES, (rc + 1) * LANES)
        right = stacked(
            *[
                jnp.concatenate([leaves[1 + i, 1 + j, c, :, cols] for i in range(2) for j in range(2)], axis=0)
                for c in range(2)
            ]
        )
        rows = min(256, total_dirs)
        for q0 in range(0, total_dirs, rows):
            left = jnp.concatenate(
                [agg[c, i, j, q0 : q0 + rows] for c in range(2) for i in range(2) for j in range(2)], axis=1
            )
            both = dot(left, right)
            for c in range(2):
                pat[c, q0 : q0 + rows, cols] = both[:, c * LANES : (c + 1) * LANES].astype(bf16)

        @pl.loop(1, owners)
        def _(i, rc=rc):
            t = lax.rem(me + i, owners)
            pltpu.make_async_remote_copy(
                src_ref=pat.at[:, dirs_of(t), lanes(rc)],
                dst_ref=grid.at[rc, 2 + s, 2 + x],
                send_sem=s1_sem.at[rc],
                recv_sem=r1_sem.at[rc, x // 2],
                device_id=owner_device(t),
                device_id_type=MESH,
            ).start()

        pltpu.make_async_copy(
            pat.at[:, dirs_of(me), lanes(rc)], grid.at[rc, 2 + s, 2 + x], r1_sem.at[rc, x // 2]
        ).start()
        if rc == 0:
            start_columns()

    start_rows((0,))

    def near(p, q, first=False):
        right = stacked(leaves[p, q, 0], leaves[p, q, 1])
        targets = [(i, j) for i in range(2) for j in range(2) if 0 <= p - i <= 2 and 0 <= q - j <= 2]
        left = jnp.concatenate(
            [
                jnp.concatenate([nb[c, i, j, 3 * (p - i) + q - j] for c in range(2)], axis=1)
                for i, j in targets
            ],
            axis=0,
        )
        both = dot(left, right)
        rows = left.shape[0] // len(targets)
        width = both.shape[1] // 2
        for n, (i, j) in enumerate(targets):
            for c in range(2):
                part = both[n * rows : (n + 1) * rows, c * width : (c + 1) * width]
                acc[c, i, j] = part if first else acc[c, i, j] + part

    loads[2].wait()
    for n, (p, q) in enumerate(((1, 1), (1, 2), (2, 1), (2, 2))):
        near(p, q, n == 0)

    @pl.when(d < nd - 1)
    def _():
        to_left.wait_recv()

    @pl.when(d > 0)
    def _():
        to_right.wait_recv()

    start_rows((1, 2))

    def plane(rc, side):
        own = grid.at[rc, 2 : ns + 2, 2:4] if side == 0 else grid.at[rc, 2 : ns + 2, nx : nx + 2]
        there = grid.at[rc, 2 : ns + 2, nx + 2 : nx + 4] if side == 0 else grid.at[rc, 2 : ns + 2, 0:2]
        return pltpu.make_async_remote_copy(
            src_ref=own, dst_ref=there, send_sem=sz_sem.at[rc, side], recv_sem=rz_sem.at[rc, side],
            device_id=(s, d - nx if side == 0 else d + nx), device_id_type=MESH,
        )

    for rc in range(2):
        for side in range(2):
            half = grid.at[rc, 2 : ns + 2, 2 + 2 * side : 4 + 2 * side]
            pltpu.make_async_copy(half, half, r1_sem.at[rc, side]).wait()

            @pl.when(z > 0 if side == 0 else z < nz - 1)
            def _(rc=rc, side=side):
                plane(rc, side).start()

        if rc == 0:
            @pl.when(s != z)
            def _():
                swap.wait_recv()

            turned = trd[...].T
            for k in range(32):
                coef[k] = jnp.broadcast_to(turned[0:nq, k : k + 1], (nq, LANES))

    for rc in range(2):

        @pl.when(z < nz - 1)
        def _(rc=rc):
            plane(rc, 0).wait_recv()

        @pl.when(z > 0)
        def _(rc=rc):
            plane(rc, 1).wait_recv()

        @pl.loop(0, ns)
        def _(target, rc=rc):
            total = [jnp.zeros((nx, nq, LANES), f32) for _ in range(2)]
            for row_step in range(-2, 3):
                term = [jnp.zeros((nx, nq, LANES), f32) for _ in range(2)]
                for k, (a, b) in enumerate(far_offsets):
                    if a == row_step:
                        u, v = (
                            grid[rc, target + 2 + a, 2 + b : 2 + b + nx, c].astype(f32) for c in range(2)
                        )
                        p, q = coef[2 * k][None], coef[2 * k + 1][None]
                        term[0] += p * u - q * v
                        term[1] += p * v + q * u
                for c in range(2):
                    total[c] += term[c].astype(bf16).astype(f32)
            for col in range(nx):
                for c in range(2):
                    inc[rc, target * nx + col, c] = total[c][col].astype(bf16)

        @pl.loop(1, owners)
        def _(i, rc=rc):
            t = lax.rem(me + i, owners)
            pltpu.make_async_remote_copy(
                src_ref=inc.at[rc, t],
                dst_ref=back.at[:, dirs_of(me), lanes(rc)],
                send_sem=s2_sem.at[rc],
                recv_sem=r2_sem.at[rc],
                device_id=owner_device(t),
                device_id_type=MESH,
            ).start()

        pltpu.make_async_copy(inc.at[rc, me], back.at[:, dirs_of(me), lanes(rc)], r2_sem.at[rc]).start()

    @pl.when(s < ns - 1)
    def _():
        for copy in up:
            copy.wait_recv()

    @pl.when(s > 0)
    def _():
        for copy in down:
            copy.wait_recv()

    for p in range(4):
        for q in range(4):
            if p in (0, 3) or q in (0, 3):
                near(p, q)

    loads[3].wait()
    outs = []
    for rc in range(2):
        cols = slice(rc * LANES, (rc + 1) * LANES)
        whole = back.at[:, :, cols]
        pltpu.make_async_copy(whole, whole, r2_sem.at[rc]).wait()
        right = stacked(back[0, :, cols], back[1, :, cols])
        for i in range(2):
            left = jnp.concatenate(
                [jnp.concatenate([dis[c, i, j] for c in range(2)], axis=1) for j in range(2)], axis=0
            )
            both = dot(left, right)
            rows = left.shape[0] // 2
            for j in range(2):
                live = live_ref[i, j].astype(f32)
                for c in range(2):
                    part = both[j * rows : (j + 1) * rows, c * LANES : (c + 1) * LANES]
                    acc[c, i, j, :, cols] = (acc[c, i, j, :, cols] + part) * live
        copy = pltpu.make_async_copy(acc.at[..., cols], out_hbm.at[..., cols], out_sem.at[rc])
        copy.start()
        outs.append(copy)

    @pl.when(s != z)
    def _():
        swap.wait_send()

    @pl.when(d > 0)
    def _():
        to_left.wait_send()

    @pl.when(d < nd - 1)
    def _():
        to_right.wait_send()

    @pl.when(s > 0)
    def _():
        for copy in up:
            copy.wait_send()

    @pl.when(s < ns - 1)
    def _():
        for copy in down:
            copy.wait_send()

    for rc in range(2):
        sent = inc.at[rc, 0 : owners - 1]
        pltpu.make_async_copy(sent, sent, s1_sem.at[rc]).wait()
        pltpu.make_async_copy(sent, sent, s2_sem.at[rc]).wait()

        @pl.when(z > 0)
        def _(rc=rc):
            plane(rc, 0).wait_send()

        @pl.when(z < nz - 1)
        def _(rc=rc):
            plane(rc, 1).wait_send()

        outs[rc].wait()


def shards(ns, nd, unknowns, leaf_live, near_blocks, aggregate, disaggregate, translate):
    nq = translate.shape[2]
    leaf, sides = unknowns.shape[3:]
    dirs = aggregate.shape[3]
    bf16, f32 = jnp.bfloat16, jnp.float32
    owners = ns * PLANE_COLS
    any_space = pl.BlockSpec(memory_space=pl.ANY)
    dma = pltpu.SemaphoreType.DMA
    field = pl.pallas_call(
        functools.partial(kernel, ns, nd),
        out_shape=jax.ShapeDtypeStruct(unknowns.shape, f32),
        in_specs=[
            pl.BlockSpec(memory_space=pltpu.SMEM),
            any_space,
            any_space,
            any_space,
            any_space,
            pl.BlockSpec(memory_space=pltpu.VMEM),
        ],
        out_specs=any_space,
        scratch_shapes=[
            pltpu.VMEM(unknowns.shape, bf16),
            pltpu.VMEM((4, 4, 2, leaf, sides), bf16),
            pltpu.VMEM(near_blocks.shape, bf16),
            pltpu.VMEM(aggregate.shape, bf16),
            pltpu.VMEM(disaggregate.shape, bf16),
            pltpu.VMEM((2, dirs, sides), bf16),
            pltpu.VMEM((2, ns + 4, PLANE_COLS + 4, 2, nq, LANES), bf16),
            pltpu.VMEM((2, owners, 2, nq, LANES), bf16),
            pltpu.VMEM((2, dirs, sides), bf16),
            pltpu.VMEM(unknowns.shape, f32),
            pltpu.VMEM((32, LANES), f32),
            pltpu.VMEM((32, LANES), f32),
            pltpu.VMEM((32, nq, LANES), f32),
            dma((4,)),
            dma((2, 2)),
            dma((2, 6)),
            dma((2, 1)),
            dma((2,)),
            dma((2, 2)),
            dma((2, 2)),
            dma((2, 2)),
            dma((2,)),
            dma((2,)),
            dma((2,)),
        ],
        compiler_params=pltpu.CompilerParams(
            collective_id=0, has_side_effects=True, vmem_limit_bytes=56 * 1024 * 1024
        ),
    )(leaf_live, unknowns, near_blocks, aggregate, disaggregate, translate)
    return field


def solution(mesh):
    in_specs = (
        P(None, "sect", "dir", None, None),
        P("sect", "dir"),
        P(None, "sect", "dir", None, None, None),
        P(None, "sect", "dir", None, None),
        P(None, "sect", "dir", None, None),
        P(None, None, "dir"),
    )
    out_specs = P(None, "sect", "dir", None, None)
    body = functools.partial(shards, mesh.shape["sect"], mesh.shape["dir"])
    return jax.shard_map(body, mesh=mesh, in_specs=in_specs, out_specs=out_specs, check_vma=False)
```

```python
import functools

import jax
import jax.numpy as jnp
from jax import lax
from jax.experimental import pallas as pl
from jax.experimental.pallas import tpu as pltpu
from jax.sharding import PartitionSpec as P

MESH = pl.DeviceIdType.MESH
PLANE_COLS = 4
LANES = 128

far_offsets = [(a, b) for a in range(-2, 3) for b in range(-2, 3) if max(abs(a), abs(b)) == 2]


def stacked(real, imag, axis=0):
    top = jnp.concatenate([real, imag], axis=1)
    low = jnp.concatenate([-imag, real], axis=1)
    return jnp.concatenate([top, low], axis=0)


def dot(left, right):
    return jnp.dot(left, right, preferred_element_type=jnp.float32)


def kernel(
    ns, nd, live_ref, unk_hbm, nb_hbm, agg_hbm, dis_hbm, tr_ref, acc,
    raw, leaves, hop, nb, agg, dis, pat, grid, inc, back, trs, trd, mix,
    load_sem, hop_sem, nx_sem, ny_sem, t_sem, s1_sem, r1_sem, sz_sem, rz_sem, s2_sem, r2_sem,
):
    nx = PLANE_COLS
    nz = nd // nx
    owners = ns * nx
    total_dirs = agg.shape[3]
    nq = total_dirs // owners
    f32, bf16 = jnp.float32, jnp.bfloat16

    s, d = lax.axis_index("sect"), lax.axis_index("dir")
    z, x = d // nx, lax.rem(d, nx)
    me = s * nx + x

    loads = [
        pltpu.make_async_copy(src, dst, load_sem.at[i])
        for i, (src, dst) in enumerate(((unk_hbm, raw), (agg_hbm, agg), (nb_hbm, nb), (dis_hbm, dis)))
    ]
    loads[0].start()
    loads[1].start()

    def owner_device(t):
        return (t // nx, z * nx + lax.rem(t, nx))

    ny = ns // 2
    y, core = s // 2, lax.rem(s, 2)
    y_order = sorted(range(ny), key=lambda step: (-min(step, ny - step), step))
    x_order = sorted(range(nx), key=lambda step: (-min(step, nx - step), step))
    y_digits = sum(step * 4**i for i, step in enumerate(y_order))

    def far_row(i):
        step = lax.rem(lax.shift_right_logical(jnp.int32(y_digits), 2 * (i // 2)), 4)
        return lax.rem(y + step, ny) * 2 + lax.rem(core + 1 + lax.rem(i, 2), 2)

    def far_columns():
        return [lax.rem(x + step, nx) for step in x_order]

    bar = pltpu.get_barrier_semaphore()

    def greet(device):
        pl.semaphore_signal(bar, inc=1, device_id=device, device_id_type=MESH)

    @pl.when(s != z)
    def _():
        greet((z, s * nx + x))

    def hops(step):
        return min(step[0], ny - step[0]) + min(step[2], nx - step[2])

    steps = [(a, b, c) for a in range(ny) for b in range(2) for c in range(nx)][1:]
    for a, b, c in sorted(steps, key=lambda step: -hops(step)):
        greet((lax.rem(y + a, ny) * 2 + lax.rem(core + b, 2), z * nx + lax.rem(x + c, nx)))
    for step in (1, nz - 1):
        greet((s, lax.rem(z + step, nz) * nx + x))

    def clear(ref):
        ref[...] = jnp.zeros(ref.shape, ref.dtype)

    @pl.when(s == 0)
    def _():
        clear(leaves.at[0])

    @pl.when(s == ns - 1)
    def _():
        clear(leaves.at[3])

    @pl.when(d == 0)
    def _():
        clear(leaves.at[1:3, 0])

    @pl.when(d == nd - 1)
    def _():
        clear(leaves.at[1:3, 3])

    clear(trs)
    for k in range(16):
        trs[2 * k : 2 * k + 2, 0:nq] = tr_ref[k]
    loads[0].wait()
    loads[2].start()
    loads[3].start()
    for i in range(2):
        for j in range(2):
            live = live_ref[i, j].astype(f32)
            for c in range(2):
                leaves[1 + i, 1 + j, c] = (raw[c, i, j].astype(f32) * live).astype(bf16)

    loads[1].wait()
    for rc in range(2):
        cols = slice(rc * LANES, (rc + 1) * LANES)
        right = stacked(
            *[
                jnp.concatenate([leaves[1 + i, 1 + j, c, :, cols] for i in range(2) for j in range(2)], axis=0)
                for c in range(2)
            ]
        )
        rows = min(256, total_dirs)
        for q0 in range(0, total_dirs, rows):
            left = jnp.concatenate(
                [agg[c, i, j, q0 : q0 + rows] for c in range(2) for i in range(2) for j in range(2)], axis=1
            )
            both = dot(left, right)
            for c in range(2):
                pat[c, q0 : q0 + rows, cols] = both[:, c * LANES : (c + 1) * LANES].astype(bf16)

    pl.semaphore_wait(bar, owners - 1 + 2 + jnp.where(s != z, 1, 0))

    def remote(src, dst, sems, i, device):
        return pltpu.make_async_remote_copy(
            src_ref=src, dst_ref=dst, send_sem=sems.at[0, i], recv_sem=sems.at[1, i],
            device_id=device, device_id_type=MESH,
        )

    swap = remote(trs, trd, t_sem, 0, (z, s * nx + x))

    @pl.when(s != z)
    def _():
        swap.start()

    @pl.when(s == z)
    def _():
        trd[...] = trs[...]

    left_end, right_end = x == 0, x == nx - 1
    before, after = z > 0, z < nz - 1
    left = (s, z * nx + jnp.where(left_end, nx - 1, x - 1))
    right = (s, z * nx + jnp.where(right_end, 0, x + 1))
    prev, nxt = (s, d - nx), (s, d + nx)

    def to_left(r, src=None):
        return remote(leaves.at[1 + r, 1] if src is None else src, leaves.at[1 + r, 3], nx_sem, r, left)

    def to_right(r, src=None):
        return remote(leaves.at[1 + r, 2] if src is None else src, leaves.at[1 + r, 0], nx_sem, 2 + r, right)

    first_left = remote(leaves.at[1, 1], hop.at[0], hop_sem, 0, prev)
    first_right = remote(leaves.at[1, 2], hop.at[0], hop_sem, 0, nxt)
    second_left = remote(leaves.at[2, 1], hop.at[1], hop_sem, 1, left)
    second_right = remote(leaves.at[2, 2], hop.at[1], hop_sem, 1, right)

    def pass_on(column, recv, device):
        return pltpu.make_async_remote_copy(
            src_ref=hop.at[1], dst_ref=leaves.at[2, column], send_sem=hop_sem.at[0, 2], recv_sem=nx_sem.at[1, recv],
            device_id=device, device_id_type=MESH,
        )


    spans = ((1, 3), (0, 1), (3, 4))
    up = [
        remote(leaves.at[1, a:b], leaves.at[3, a:b], ny_sem, i, (s - 1, d)) for i, (a, b) in enumerate(spans)
    ]
    down = [
        remote(leaves.at[2, a:b], leaves.at[0, a:b], ny_sem, 3 + i, (s + 1, d)) for i, (a, b) in enumerate(spans)
    ]

    def start_columns():
        for r in range(2):

            @pl.when(jnp.logical_not(left_end))
            def _(r=r):
                to_left(r).start()

            @pl.when(jnp.logical_not(right_end))
            def _(r=r):
                to_right(r).start()

        @pl.when(left_end & before)
        def _():
            second_left.start()

        @pl.when(right_end & after)
        def _():
            second_right.start()

    def start_hops():
        @pl.when(left_end & before)
        def _():
            first_left.start()

        @pl.when(right_end & after)
        def _():
            first_right.start()

    def pass_first():
        @pl.when(left_end & after)
        def _():
            first_left.wait_recv()
            to_left(0, hop.at[0]).start()

        @pl.when(right_end & before)
        def _():
            first_right.wait_recv()
            to_right(0, hop.at[0]).start()

    def pass_second():
        @pl.when(right_end & before)
        def _():
            second_left.wait_recv()
            pass_on(3, 1, prev).start()

        @pl.when(left_end & after)
        def _():
            second_right.wait_recv()
            pass_on(0, 3, nxt).start()

    def columns_came(r):
        @pl.when(d < nd - 1)
        def _():
            to_left(r).wait_recv()

        @pl.when(d > 0)
        def _():
            to_right(r).wait_recv()

    def start_up(which):
        @pl.when(s > 0)
        def _():
            for i in which:
                up[i].start()

    def start_down(which):
        @pl.when(s < ns - 1)
        def _():
            for i in which:
                down[i].start()

    def lanes(rc):
        return pl.ds(rc * LANES, LANES)

    def dirs_of(t):
        return pl.ds(pl.multiple_of(t * nq, nq), nq)

    start_hops()

    for rc in range(2):

        @pl.loop(0, ns)
        def _(i, rc=rc):
            row = far_row(i)
            for col in far_columns():
                t = row * nx + col
                src, dst = pat.at[:, dirs_of(t), lanes(rc)], grid.at[rc, 2 + s, 2 + x]
                arrived = r1_sem.at[rc, x // 2, y]

                @pl.when(t != me)
                def _(t=t, src=src):
                    pltpu.make_async_remote_copy(
                        src_ref=src, dst_ref=dst, send_sem=s1_sem.at[rc], recv_sem=arrived,
                        device_id=owner_device(t), device_id_type=MESH,
                    ).start()

                @pl.when(t == me)
                def _(src=src):
                    pltpu.make_async_copy(src, dst, arrived).start()

    start_columns()
    start_up((0,))
    start_down((0,))
    for rc in range(2):
        clear(grid.at[rc, 0:2])
        clear(grid.at[rc, ns + 2 : ns + 4])

    @pl.when(z == 0)
    def _():
        for rc in range(2):
            clear(grid.at[rc, 2 : ns + 2, 0:2])

    @pl.when(z == nz - 1)
    def _():
        for rc in range(2):
            clear(grid.at[rc, 2 : ns + 2, nx + 2 : nx + 4])

    def near(p, q, first=False):
        right = stacked(leaves[p, q, 0], leaves[p, q, 1])
        targets = [(i, j) for i in range(2) for j in range(2) if 0 <= p - i <= 2 and 0 <= q - j <= 2]
        left = jnp.concatenate(
            [
                jnp.concatenate([nb[c, i, j, 3 * (p - i) + q - j] for c in range(2)], axis=1)
                for i, j in targets
            ],
            axis=0,
        )
        both = dot(left, right)
        rows = left.shape[0] // len(targets)
        width = both.shape[1] // 2
        for n, (i, j) in enumerate(targets):
            for c in range(2):
                part = both[n * rows : (n + 1) * rows, c * width : (c + 1) * width]
                acc[c, i, j] = part if first else acc[c, i, j] + part

    loads[2].wait()
    for n, (p, q) in enumerate(((1, 1), (1, 2), (2, 1), (2, 2))):
        near(p, q, n == 0)

    def plane(rc, side, first, count):
        rows = pl.ds(2 + first, count)
        own = grid.at[rc, rows, 2:4] if side == 0 else grid.at[rc, rows, nx : nx + 2]
        there = grid.at[rc, rows, nx + 2 : nx + 4] if side == 0 else grid.at[rc, rows, 0:2]
        return pltpu.make_async_remote_copy(
            src_ref=own, dst_ref=there, send_sem=sz_sem.at[rc, side], recv_sem=rz_sem.at[rc, side],
            device_id=(s, d - nx if side == 0 else d + nx), device_id_type=MESH,
        )

    for rc in range(2):
        for step in y_order:
            from_y = lax.rem(y + step, ny)
            for side in range(2):
                part = grid.at[rc, pl.ds(2 + 2 * from_y, 2), 2 + 2 * side : 4 + 2 * side]
                pltpu.make_async_copy(part, part, r1_sem.at[rc, side, from_y]).wait()

                @pl.when(z > 0 if side == 0 else z < nz - 1)
                def _(rc=rc, side=side, from_y=from_y):
                    plane(rc, side, 2 * from_y, 2).start()

        if rc == 0:
            pass_first()
            @pl.when(s != z)
            def _():
                swap.wait_recv()

            turned = trd[...].T
            wide = mix.shape[2]
            lane = lax.broadcasted_iota(jnp.int32, (nq, wide), 1)
            same = lax.rem(lane, nq) == lax.broadcasted_iota(jnp.int32, (nq, wide), 0)
            imag = lax.rem(lane // nq, 2) == 1
            source = jnp.where(same, lane // (2 * nq), -1)
            for row_step in range(-2, 3):
                ks = [(k, b) for k, (a, b) in enumerate(far_offsets) if a == row_step]
                for c in range(2):
                    rows = [jnp.zeros((nq, wide), f32) for _ in range(nx)]
                    for k, b in ks:
                        p, q = (jnp.broadcast_to(turned[0:nq, 2 * k + n : 2 * k + n + 1], (nq, wide)) for n in range(2))
                        value = jnp.where(imag, p, q) if c else jnp.where(imag, -q, p)
                        rows = [jnp.where(source == 2 + col + b, value, rows[col]) for col in range(nx)]
                    for col in range(nx):
                        first = (2 * col + c) * nq
                        mix[row_step + 2, first : first + nq] = rows[col].astype(bf16)

    for rc in range(2):

        @pl.when(z < nz - 1)
        def _(rc=rc):
            plane(rc, 0, 0, ns).wait_recv()

        @pl.when(z > 0)
        def _(rc=rc):
            plane(rc, 1, 0, ns).wait_recv()

        @pl.loop(0, ny)
        def _(i, rc=rc):
            first = 2 * lax.rem(y + lax.rem(lax.shift_right_logical(jnp.int32(y_digits), 2 * i), 4), ny)
            total = jnp.zeros((2 * nx * nq, 2 * LANES), f32)
            for row_step in range(5):
                right = jnp.concatenate(
                    [grid[rc, first + n + row_step].reshape(2 * (nx + 4) * nq, LANES) for n in range(2)], axis=1
                )
                total += dot(mix[row_step], right).astype(bf16).astype(f32)
            for n in range(2):
                inc[rc, pl.ds((first + n) * nx, nx)] = (
                    total[:, n * LANES : (n + 1) * LANES].astype(bf16).reshape(nx, 2, nq, LANES)
                )
            for col in far_columns():
                for n in range(2):
                    t = (first + n) * nx + col
                    src, dst = inc.at[rc, t], back.at[:, dirs_of(me), lanes(rc)]

                    @pl.when(t != me)
                    def _(t=t, src=src):
                        pltpu.make_async_remote_copy(
                            src_ref=src, dst_ref=dst, send_sem=s2_sem.at[rc], recv_sem=r2_sem.at[rc],
                            device_id=owner_device(t), device_id_type=MESH,
                        ).start()

                    @pl.when(t == me)
                    def _(src=src):
                        pltpu.make_async_copy(src, dst, r2_sem.at[rc]).start()

        if rc == 0:
            pass_second()
            columns_came(0)
            start_up((1, 2))
        else:
            columns_came(1)
            start_down((1, 2))

    @pl.when(s < ns - 1)
    def _():
        for copy in up:
            copy.wait_recv()

    @pl.when(s > 0)
    def _():
        for copy in down:
            copy.wait_recv()

    for p in range(4):
        for q in range(4):
            if p in (0, 3) or q in (0, 3):
                near(p, q)

    loads[3].wait()
    for rc in range(2):
        cols = slice(rc * LANES, (rc + 1) * LANES)
        whole = back.at[:, :, cols]
        pltpu.make_async_copy(whole, whole, r2_sem.at[rc]).wait()
        right = stacked(back[0, :, cols], back[1, :, cols])
        for i in range(2):
            left = jnp.concatenate(
                [jnp.concatenate([dis[c, i, j] for c in range(2)], axis=1) for j in range(2)], axis=0
            )
            both = dot(left, right)
            rows = left.shape[0] // 2
            for j in range(2):
                live = live_ref[i, j].astype(f32)
                for c in range(2):
                    part = both[j * rows : (j + 1) * rows, c * LANES : (c + 1) * LANES]
                    acc[c, i, j, :, cols] = (acc[c, i, j, :, cols] + part) * live

    @pl.when(s != z)
    def _():
        swap.wait_send()

    @pl.when(jnp.logical_not(left_end) | after)
    def _():
        to_left(0).wait_send()

    @pl.when(jnp.logical_not(right_end) | before)
    def _():
        to_right(0).wait_send()

    @pl.when(jnp.logical_not(left_end))
    def _():
        to_left(1).wait_send()

    @pl.when(jnp.logical_not(right_end))
    def _():
        to_right(1).wait_send()

    @pl.when(left_end & before | right_end & after)
    def _():
        first_left.wait_send()
        second_left.wait_send()

    @pl.when(right_end & before | left_end & after)
    def _():
        pass_on(3, 1, prev).wait_send()

    @pl.when(s > 0)
    def _():
        for copy in up:
            copy.wait_send()

    @pl.when(s < ns - 1)
    def _():
        for copy in down:
            copy.wait_send()

    for rc in range(2):
        sent = inc.at[rc, 0 : owners - 1]
        pltpu.make_async_copy(sent, sent, s1_sem.at[rc]).wait()
        pltpu.make_async_copy(sent, sent, s2_sem.at[rc]).wait()

        @pl.when(z > 0)
        def _(rc=rc):
            plane(rc, 0, 0, ns).wait_send()

        @pl.when(z < nz - 1)
        def _(rc=rc):
            plane(rc, 1, 0, ns).wait_send()


def shards(ns, nd, unknowns, leaf_live, near_blocks, aggregate, disaggregate, translate):
    nq = translate.shape[2]
    leaf, sides = unknowns.shape[3:]
    dirs = aggregate.shape[3]
    bf16, f32 = jnp.bfloat16, jnp.float32
    owners = ns * PLANE_COLS
    any_space = pl.BlockSpec(memory_space=pl.ANY)
    dma = pltpu.SemaphoreType.DMA
    field = pl.pallas_call(
        functools.partial(kernel, ns, nd),
        out_shape=pltpu.VMEM(unknowns.shape, f32),
        in_specs=[
            pl.BlockSpec(memory_space=pltpu.SMEM),
            any_space,
            any_space,
            any_space,
            any_space,
            pl.BlockSpec(memory_space=pltpu.VMEM),
        ],
        out_specs=pl.BlockSpec(memory_space=pltpu.VMEM),
        scratch_shapes=[
            pltpu.VMEM(unknowns.shape, bf16),
            pltpu.VMEM((4, 4, 2, leaf, sides), bf16),
            pltpu.VMEM((2, 2, leaf, sides), bf16),
            pltpu.VMEM(near_blocks.shape, bf16),
            pltpu.VMEM(aggregate.shape, bf16),
            pltpu.VMEM(disaggregate.shape, bf16),
            pltpu.VMEM((2, dirs, sides), bf16),
            pltpu.VMEM((2, ns + 4, PLANE_COLS + 4, 2, nq, LANES), bf16),
            pltpu.VMEM((2, owners, 2, nq, LANES), bf16),
            pltpu.VMEM((2, dirs, sides), bf16),
            pltpu.VMEM((32, LANES), f32),
            pltpu.VMEM((32, LANES), f32),
            pltpu.VMEM((5, 2 * PLANE_COLS * nq, 2 * (PLANE_COLS + 4) * nq), bf16),
            dma((4,)),
            dma((2, 3)),
            dma((2, 4)),
            dma((2, 6)),
            dma((2, 1)),
            dma((2,)),
            dma((2, 2, ns // 2)),
            dma((2, 2)),
            dma((2, 2)),
            dma((2,)),
            dma((2,)),
        ],
        compiler_params=pltpu.CompilerParams(
            collective_id=0, has_side_effects=True, vmem_limit_bytes=56 * 1024 * 1024
        ),
    )(leaf_live, unknowns, near_blocks, aggregate, disaggregate, translate)
    return field


def solution(mesh):
    in_specs = (
        P(None, "sect", "dir", None, None),
        P("sect", "dir"),
        P(None, "sect", "dir", None, None, None),
        P(None, "sect", "dir", None, None),
        P(None, "sect", "dir", None, None),
        P(None, None, "dir"),
    )
    out_specs = P(None, "sect", "dir", None, None)
    body = functools.partial(shards, mesh.shape["sect"], mesh.shape["dir"])
    return jax.shard_map(body, mesh=mesh, in_specs=in_specs, out_specs=out_specs, check_vma=False)
```

```python
import functools

import jax
import jax.numpy as jnp
from jax import lax
from jax.experimental import pallas as pl
from jax.experimental.pallas import tpu as pltpu
from jax.sharding import PartitionSpec as P

MESH = pl.DeviceIdType.MESH
PLANE_COLS = 4
LANES = 128

far_offsets = [(a, b) for a in range(-2, 3) for b in range(-2, 3) if max(abs(a), abs(b)) == 2]


def stacked(real, imag, axis=0):
    top = jnp.concatenate([real, imag], axis=1)
    low = jnp.concatenate([-imag, real], axis=1)
    return jnp.concatenate([top, low], axis=0)


def dot(left, right):
    return jnp.dot(left, right, preferred_element_type=jnp.float32)


def kernel(
    ns, nd, live_ref, unk_hbm, nb_hbm, agg_hbm, dis_hbm, tr_ref, acc,
    raw, leaves, hop, nb, agg, dis, pat, grid, inc, back, trs, trd, mix,
    load_sem, hop_sem, nx_sem, ny_sem, t_sem, s1_sem, r1_sem, sz_sem, rz_sem, s2_sem, r2_sem,
):
    nx = PLANE_COLS
    nz = nd // nx
    owners = ns * nx
    total_dirs = agg.shape[3]
    nq = total_dirs // owners
    f32, bf16 = jnp.float32, jnp.bfloat16

    s, d = lax.axis_index("sect"), lax.axis_index("dir")
    z, x = d // nx, lax.rem(d, nx)
    me = s * nx + x

    loads = [
        pltpu.make_async_copy(src, dst, load_sem.at[i])
        for i, (src, dst) in enumerate(((unk_hbm, raw), (agg_hbm, agg), (nb_hbm, nb), (dis_hbm, dis)))
    ]
    loads[0].start()
    loads[1].start()

    ny = ns // 2
    y, core = s // 2, lax.rem(s, 2)
    y_order = sorted(range(ny), key=lambda step: (-min(step, ny - step), step))
    x_order = sorted(range(nx), key=lambda step: (-min(step, nx - step), step))
    y_digits = sum(step * 4**i for i, step in enumerate(y_order))
    cores = (1 - core, core)

    def y_at(i):
        return lax.rem(y + lax.rem(lax.shift_right_logical(jnp.int32(y_digits), 2 * i), 4), ny)

    columns = [lax.rem(x + step, nx) for step in x_order]

    def send(src, dst, row, col, send_sem, recv_sem):
        pltpu.make_async_remote_copy(
            src_ref=src, dst_ref=dst, send_sem=send_sem, recv_sem=recv_sem,
            device_id=(row, z * nx + col), device_id_type=MESH,
        ).start()

    bar = pltpu.get_barrier_semaphore()

    def greet(device):
        pl.semaphore_signal(bar, inc=1, device_id=device, device_id_type=MESH)

    @pl.when(s != z)
    def _():
        greet((z, s * nx + x))

    def hops(step):
        return min(step[0], ny - step[0]) + min(step[2], nx - step[2])

    steps = [(a, b, c) for a in range(ny) for b in range(2) for c in range(nx)][1:]
    for a, b, c in sorted(steps, key=lambda step: -hops(step)):
        greet((lax.rem(y + a, ny) * 2 + lax.rem(core + b, 2), z * nx + lax.rem(x + c, nx)))
    for step in (1, nz - 1):
        greet((s, lax.rem(z + step, nz) * nx + x))

    def clear(ref):
        ref[...] = jnp.zeros(ref.shape, ref.dtype)

    @pl.when(s == 0)
    def _():
        clear(leaves.at[0])

    @pl.when(s == ns - 1)
    def _():
        clear(leaves.at[3])

    @pl.when(d == 0)
    def _():
        clear(leaves.at[1:3, 0])

    @pl.when(d == nd - 1)
    def _():
        clear(leaves.at[1:3, 3])

    clear(trs)
    for k in range(16):
        trs[2 * k : 2 * k + 2, 0:nq] = tr_ref[k]
    loads[0].wait()
    loads[2].start()
    loads[3].start()
    for i in range(2):
        for j in range(2):
            live = live_ref[i, j].astype(f32)
            for c in range(2):
                leaves[1 + i, 1 + j, c] = (raw[c, i, j].astype(f32) * live).astype(bf16)

    loads[1].wait()
    rows = min(256, total_dirs)
    for rc in range(2):
        cols = slice(rc * LANES, (rc + 1) * LANES)

        @pl.loop(0, total_dirs // rows)
        def _(n, rc=rc, cols=cols):
            right = stacked(
                *[
                    jnp.concatenate([leaves[1 + i, 1 + j, c, :, cols] for i in range(2) for j in range(2)], axis=0)
                    for c in range(2)
                ]
            )
            some = pl.ds(pl.multiple_of(n * rows, rows), rows)
            left = jnp.concatenate(
                [agg[c, i, j, some] for c in range(2) for i in range(2) for j in range(2)], axis=1
            )
            both = dot(left, right)
            for c in range(2):
                pat[rc, pl.ds(n * (rows // nq), rows // nq), c] = (
                    both[:, c * LANES : (c + 1) * LANES].astype(bf16).reshape(rows // nq, nq, LANES)
                )

    acc[...] = jnp.zeros(acc.shape, f32)
    pl.semaphore_wait(bar, owners - 1 + 2 + jnp.where(s != z, 1, 0))

    def remote(src, dst, sems, i, device):
        return pltpu.make_async_remote_copy(
            src_ref=src, dst_ref=dst, send_sem=sems.at[0, i], recv_sem=sems.at[1, i],
            device_id=device, device_id_type=MESH,
        )

    swap = remote(trs, trd, t_sem, 0, (z, s * nx + x))

    @pl.when(s != z)
    def _():
        swap.start()

    @pl.when(s == z)
    def _():
        trd[...] = trs[...]

    left_end, right_end = x == 0, x == nx - 1
    before, after = z > 0, z < nz - 1
    left = (s, z * nx + jnp.where(left_end, nx - 1, x - 1))
    right = (s, z * nx + jnp.where(right_end, 0, x + 1))
    prev, nxt = (s, d - nx), (s, d + nx)

    def to_left(r, src=None):
        return remote(leaves.at[1 + r, 1] if src is None else src, leaves.at[1 + r, 3], nx_sem, r, left)

    def to_right(r, src=None):
        return remote(leaves.at[1 + r, 2] if src is None else src, leaves.at[1 + r, 0], nx_sem, 2 + r, right)

    first_left = remote(leaves.at[1, 1], hop.at[0], hop_sem, 0, prev)
    first_right = remote(leaves.at[1, 2], hop.at[0], hop_sem, 0, nxt)
    second_left = remote(leaves.at[2, 1], hop.at[1], hop_sem, 1, left)
    second_right = remote(leaves.at[2, 2], hop.at[1], hop_sem, 1, right)

    def pass_on(column, recv, device):
        return pltpu.make_async_remote_copy(
            src_ref=hop.at[1], dst_ref=leaves.at[2, column], send_sem=hop_sem.at[0, 2], recv_sem=nx_sem.at[1, recv],
            device_id=device, device_id_type=MESH,
        )


    spans = ((1, 3), (0, 1), (3, 4))
    up = [
        remote(leaves.at[1, a:b], leaves.at[3, a:b], ny_sem, i, (s - 1, d)) for i, (a, b) in enumerate(spans)
    ]
    down = [
        remote(leaves.at[2, a:b], leaves.at[0, a:b], ny_sem, 3 + i, (s + 1, d)) for i, (a, b) in enumerate(spans)
    ]

    def start_columns():
        for r in range(2):

            @pl.when(jnp.logical_not(left_end))
            def _(r=r):
                to_left(r).start()

            @pl.when(jnp.logical_not(right_end))
            def _(r=r):
                to_right(r).start()

        @pl.when(left_end & before)
        def _():
            second_left.start()

        @pl.when(right_end & after)
        def _():
            second_right.start()

    def start_hops():
        @pl.when(left_end & before)
        def _():
            first_left.start()

        @pl.when(right_end & after)
        def _():
            first_right.start()

    def pass_first():
        @pl.when(left_end & after)
        def _():
            first_left.wait_recv()
            to_left(0, hop.at[0]).start()

        @pl.when(right_end & before)
        def _():
            first_right.wait_recv()
            to_right(0, hop.at[0]).start()

    def pass_second():
        @pl.when(right_end & before)
        def _():
            second_left.wait_recv()
            pass_on(3, 1, prev).start()

        @pl.when(left_end & after)
        def _():
            second_right.wait_recv()
            pass_on(0, 3, nxt).start()

    def columns_came(r):
        @pl.when(d < nd - 1)
        def _():
            to_left(r).wait_recv()

        @pl.when(d > 0)
        def _():
            to_right(r).wait_recv()

    def start_up(which):
        @pl.when(s > 0)
        def _():
            for i in which:
                up[i].start()

    def start_down(which):
        @pl.when(s < ns - 1)
        def _():
            for i in which:
                down[i].start()

    start_hops()

    @pl.loop(0, 2)
    def _(rc):
        dst, arrived = grid.at[rc, 2 + s, 2 + x], r1_sem.at[rc, x // 2, y]
        for y_step in y_order:
            for n, other in enumerate(cores):
                row = 2 * lax.rem(y + y_step, ny) + other
                for x_step, col in zip(x_order, columns):
                    if y_step or x_step or n == 0:
                        send(pat.at[rc, row * nx + col], dst, row, col, s1_sem.at[rc], arrived)
        pltpu.make_async_copy(pat.at[rc, me], dst, arrived).start()

    start_columns()
    start_up((0,))
    start_down((0,))
    for rc in range(2):
        clear(grid.at[rc, 0:2])
        clear(grid.at[rc, ns + 2 : ns + 4])

    @pl.when(z == 0)
    def _():
        for rc in range(2):
            clear(grid.at[rc, 2 : ns + 2, 0:2])

    @pl.when(z == nz - 1)
    def _():
        for rc in range(2):
            clear(grid.at[rc, 2 : ns + 2, nx + 2 : nx + 4])

    def near(p, q):
        targets = [(i, j) for i in range(2) for j in range(2) if 0 <= p - i <= 2 and 0 <= q - j <= 2]
        right = stacked(leaves[p, q, 0], leaves[p, q, 1])
        left = jnp.concatenate(
            [
                jnp.concatenate([nb[c, i, j, 3 * (p - i) + q - j] for c in range(2)], axis=1)
                for i, j in targets
            ],
            axis=0,
        )
        both = dot(left, right)
        rows = left.shape[0] // len(targets)
        width = both.shape[1] // 2
        for n, (i, j) in enumerate(targets):
            for c in range(2):
                acc[c, i, j] += both[n * rows : (n + 1) * rows, c * width : (c + 1) * width]

    loads[2].wait()

    for p in range(1, 3):
        for q in range(1, 3):
            near(p, q)

    def plane(rc, side, first, count):
        rows = pl.ds(2 + first, count)
        own = grid.at[rc, rows, 2:4] if side == 0 else grid.at[rc, rows, nx : nx + 2]
        there = grid.at[rc, rows, nx + 2 : nx + 4] if side == 0 else grid.at[rc, rows, 0:2]
        return pltpu.make_async_remote_copy(
            src_ref=own, dst_ref=there, send_sem=sz_sem.at[rc, side], recv_sem=rz_sem.at[rc, side],
            device_id=(s, d - nx if side == 0 else d + nx), device_id_type=MESH,
        )

    for rc in range(2):
        @pl.loop(0, ny)
        def _(i, rc=rc):
            from_y = y_at(i)
            for side in range(2):
                part = grid.at[rc, pl.ds(2 + 2 * from_y, 2), 2 + 2 * side : 4 + 2 * side]
                pltpu.make_async_copy(part, part, r1_sem.at[rc, side, from_y]).wait()

                @pl.when(z > 0 if side == 0 else z < nz - 1)
                def _(rc=rc, side=side, from_y=from_y):
                    plane(rc, side, 2 * from_y, 2).start()

        if rc == 0:
            pass_first()
            @pl.when(s != z)
            def _():
                swap.wait_recv()

            turned = trd[...].T
            half, wide = mix.shape[1] // 2, mix.shape[2]
            lane = lax.broadcasted_iota(jnp.int32, (nq, wide), 1)
            same = lax.rem(lane, nq) == lax.broadcasted_iota(jnp.int32, (nq, wide), 0)
            imag = lax.rem(lane // nq, 2) == 1
            source = jnp.where(same, lane // (2 * nq), -1)
            for row_step in range(-2, 3):
                ks = [(k, b) for k, (a, b) in enumerate(far_offsets) if a == row_step]
                for c in range(2):
                    rows = [jnp.zeros((nq, wide), f32) for _ in range(nx)]
                    for k, b in ks:
                        p, q = (jnp.broadcast_to(turned[0:nq, 2 * k + n : 2 * k + n + 1], (nq, wide)) for n in range(2))
                        value = jnp.where(imag, p, q) if c else jnp.where(imag, -q, p)
                        rows = [jnp.where(source == 2 + col + b, value, rows[col]) for col in range(nx)]
                    for col in range(nx):
                        first = (2 * col + c) * nq
                        high = rows[col].astype(bf16)
                        mix[row_step + 2, first : first + nq] = high
                        rest = (rows[col] - high.astype(f32)).astype(bf16)
                        mix[row_step + 2, half + first : half + first + nq] = rest

    for rc in range(2):

        @pl.when(z < nz - 1)
        def _(rc=rc):
            plane(rc, 0, 0, ns).wait_recv()

        @pl.when(z > 0)
        def _(rc=rc):
            plane(rc, 1, 0, ns).wait_recv()

        @pl.loop(0, ny)
        def _(i, rc=rc):
            first = 2 * y_at(i)
            total = jnp.zeros((2 * nx * nq, 2 * LANES), f32)
            for row_step in range(5):
                right = jnp.concatenate(
                    [grid[rc, first + n + row_step].reshape(2 * (nx + 4) * nq, LANES) for n in range(2)], axis=1
                )
                term = dot(mix[row_step], right)
                total += (term[: 2 * nx * nq] + term[2 * nx * nq :]).astype(bf16).astype(f32)
            for n in range(2):
                inc[rc, pl.ds((first + n) * nx, nx)] = (
                    total[:, n * LANES : (n + 1) * LANES].astype(bf16).reshape(nx, 2, nq, LANES)
                )
            dst = back.at[rc, me]
            for n, other in enumerate(cores):
                row = first + other
                for x_step, col in zip(x_order, columns):
                    src, sems = inc.at[rc, row * nx + col], (s2_sem.at[rc], r2_sem.at[rc])
                    if n == 0 or x_step:
                        send(src, dst, row, col, *sems)
                        continue

                    @pl.when(i < ny - 1)
                    def _(src=src, row=row, col=col, sems=sems):
                        send(src, dst, row, col, *sems)

                    @pl.when(i == ny - 1)
                    def _(src=src, sems=sems):
                        pltpu.make_async_copy(src, dst, sems[1]).start()

        if rc == 0:
            pass_second()
            columns_came(0)
            start_up((1, 2))
        else:
            columns_came(1)
            start_down((1, 2))

    @pl.when(s < ns - 1)
    def _():
        for copy in up:
            copy.wait_recv()

    @pl.when(s > 0)
    def _():
        for copy in down:
            copy.wait_recv()

    for p in range(4):
        for q in range(4):
            if p in (0, 3) or q in (0, 3):
                near(p, q)

    loads[3].wait()
    for rc in range(2):
        cols = slice(rc * LANES, (rc + 1) * LANES)
        whole = back.at[rc]
        pltpu.make_async_copy(whole, whole, r2_sem.at[rc]).wait()
        right = stacked(*[back[rc, :, c].reshape(owners * nq, LANES) for c in range(2)])
        for i in range(2):
            left = jnp.concatenate(
                [jnp.concatenate([dis[c, i, j] for c in range(2)], axis=1) for j in range(2)], axis=0
            )
            both = dot(left, right)
            rows = left.shape[0] // 2
            for j in range(2):
                live = live_ref[i, j].astype(f32)
                for c in range(2):
                    part = both[j * rows : (j + 1) * rows, c * LANES : (c + 1) * LANES]
                    acc[c, i, j, :, cols] = (acc[c, i, j, :, cols] + part) * live

    @pl.when(s != z)
    def _():
        swap.wait_send()

    @pl.when(jnp.logical_not(left_end) | after)
    def _():
        to_left(0).wait_send()

    @pl.when(jnp.logical_not(right_end) | before)
    def _():
        to_right(0).wait_send()

    @pl.when(jnp.logical_not(left_end))
    def _():
        to_left(1).wait_send()

    @pl.when(jnp.logical_not(right_end))
    def _():
        to_right(1).wait_send()

    @pl.when(left_end & before | right_end & after)
    def _():
        first_left.wait_send()
        second_left.wait_send()

    @pl.when(right_end & before | left_end & after)
    def _():
        pass_on(3, 1, prev).wait_send()

    @pl.when(s > 0)
    def _():
        for copy in up:
            copy.wait_send()

    @pl.when(s < ns - 1)
    def _():
        for copy in down:
            copy.wait_send()

    for rc in range(2):
        sent = inc.at[rc, 0 : owners - 1]
        pltpu.make_async_copy(sent, sent, s1_sem.at[rc]).wait()
        pltpu.make_async_copy(sent, sent, s2_sem.at[rc]).wait()

        @pl.when(z > 0)
        def _(rc=rc):
            plane(rc, 0, 0, ns).wait_send()

        @pl.when(z < nz - 1)
        def _(rc=rc):
            plane(rc, 1, 0, ns).wait_send()


def shards(ns, nd, unknowns, leaf_live, near_blocks, aggregate, disaggregate, translate):
    nq = translate.shape[2]
    leaf, sides = unknowns.shape[3:]
    dirs = aggregate.shape[3]
    bf16, f32 = jnp.bfloat16, jnp.float32
    owners = ns * PLANE_COLS
    any_space = pl.BlockSpec(memory_space=pl.ANY)
    dma = pltpu.SemaphoreType.DMA
    field = pl.pallas_call(
        functools.partial(kernel, ns, nd),
        out_shape=pltpu.VMEM(unknowns.shape, f32),
        in_specs=[
            pl.BlockSpec(memory_space=pltpu.SMEM),
            any_space,
            any_space,
            any_space,
            any_space,
            pl.BlockSpec(memory_space=pltpu.VMEM),
        ],
        out_specs=pl.BlockSpec(memory_space=pltpu.VMEM),
        scratch_shapes=[
            pltpu.VMEM(unknowns.shape, bf16),
            pltpu.VMEM((4, 4, 2, leaf, sides), bf16),
            pltpu.VMEM((2, 2, leaf, sides), bf16),
            pltpu.VMEM(near_blocks.shape, bf16),
            pltpu.VMEM(aggregate.shape, bf16),
            pltpu.VMEM(disaggregate.shape, bf16),
            pltpu.VMEM((2, owners, 2, nq, LANES), bf16),
            pltpu.VMEM((2, ns + 4, PLANE_COLS + 4, 2, nq, LANES), bf16),
            pltpu.VMEM((2, owners, 2, nq, LANES), bf16),
            pltpu.VMEM((2, owners, 2, nq, LANES), bf16),
            pltpu.VMEM((32, LANES), f32),
            pltpu.VMEM((32, LANES), f32),
            pltpu.VMEM((5, 4 * PLANE_COLS * nq, 2 * (PLANE_COLS + 4) * nq), bf16),
            dma((4,)),
            dma((2, 3)),
            dma((2, 4)),
            dma((2, 6)),
            dma((2, 1)),
            dma((2,)),
            dma((2, 2, ns // 2)),
            dma((2, 2)),
            dma((2, 2)),
            dma((2,)),
            dma((2,)),
        ],
        compiler_params=pltpu.CompilerParams(
            collective_id=0, has_side_effects=True, vmem_limit_bytes=56 * 1024 * 1024
        ),
    )(leaf_live, unknowns, near_blocks, aggregate, disaggregate, translate)
    return field


def solution(mesh):
    in_specs = (
        P(None, "sect", "dir", None, None),
        P("sect", "dir"),
        P(None, "sect", "dir", None, None, None),
        P(None, "sect", "dir", None, None),
        P(None, "sect", "dir", None, None),
        P(None, None, "dir"),
    )
    out_specs = P(None, "sect", "dir", None, None)
    body = functools.partial(shards, mesh.shape["sect"], mesh.shape["dir"])
    return jax.shard_map(body, mesh=mesh, in_specs=in_specs, out_specs=out_specs, check_vma=False)
```

```python
import functools

import jax
import jax.numpy as jnp
from jax import lax
from jax.experimental import pallas as pl
from jax.experimental.pallas import tpu as pltpu
from jax.sharding import PartitionSpec as P

MESH = pl.DeviceIdType.MESH
PLANE_COLS = 4
LANES = 128

far_offsets = [(a, b) for a in range(-2, 3) for b in range(-2, 3) if max(abs(a), abs(b)) == 2]


def stacked(real, imag, axis=0):
    top = jnp.concatenate([real, imag], axis=1)
    low = jnp.concatenate([-imag, real], axis=1)
    return jnp.concatenate([top, low], axis=0)


def dot(left, right):
    return jnp.dot(left, right, preferred_element_type=jnp.float32)


def kernel(
    ns, nd, live_ref, unk_hbm, nb_hbm, agg_hbm, dis_hbm, tr_ref, acc,
    raw, leaves, hop, nb, agg, dis, pat, grid, inc, back, trs, trd, mix,
    load_sem, hop_sem, nx_sem, ny_sem, t_sem, s1_sem, r1_sem, sz_sem, rz_sem, s2_sem, r2_sem,
):
    nx = PLANE_COLS
    nz = nd // nx
    owners = ns * nx
    total_dirs = agg.shape[3]
    nq = total_dirs // owners
    f32, bf16 = jnp.float32, jnp.bfloat16

    s, d = lax.axis_index("sect"), lax.axis_index("dir")
    z, x = d // nx, lax.rem(d, nx)
    me = s * nx + x

    loads = [
        pltpu.make_async_copy(src, dst, load_sem.at[i])
        for i, (src, dst) in enumerate(((unk_hbm, raw), (agg_hbm, agg), (nb_hbm, nb), (dis_hbm, dis)))
    ]
    loads[0].start()
    loads[1].start()

    ny = ns // 2
    y, core = s // 2, lax.rem(s, 2)
    y_order = sorted(range(ny), key=lambda step: (-min(step, ny - step), step))
    x_order = sorted(range(nx), key=lambda step: (-min(step, nx - step), step))
    y_digits = sum(step * 4**i for i, step in enumerate(y_order))
    cores = (1 - core, core)

    def y_at(i):
        return lax.rem(y + lax.rem(lax.shift_right_logical(jnp.int32(y_digits), 2 * i), 4), ny)

    columns = [lax.rem(x + step, nx) for step in x_order]

    def send(src, dst, row, col, send_sem, recv_sem):
        pltpu.make_async_remote_copy(
            src_ref=src, dst_ref=dst, send_sem=send_sem, recv_sem=recv_sem,
            device_id=(row, z * nx + col), device_id_type=MESH,
        ).start()

    bar = pltpu.get_barrier_semaphore()

    def greet(device):
        pl.semaphore_signal(bar, inc=1, device_id=device, device_id_type=MESH)

    @pl.when(s != z)
    def _():
        greet((z, s * nx + x))

    def hops(step):
        return min(step[0], ny - step[0]) + min(step[2], nx - step[2])

    steps = [(a, b, c) for a in range(ny) for b in range(2) for c in range(nx)][1:]
    for a, b, c in sorted(steps, key=lambda step: -hops(step)):
        greet((lax.rem(y + a, ny) * 2 + lax.rem(core + b, 2), z * nx + lax.rem(x + c, nx)))
    for step in (1, nz - 1):
        greet((s, lax.rem(z + step, nz) * nx + x))

    def clear(ref):
        ref[...] = jnp.zeros(ref.shape, ref.dtype)

    @pl.when(s == 0)
    def _():
        clear(leaves.at[0])

    @pl.when(s == ns - 1)
    def _():
        clear(leaves.at[3])

    @pl.when(d == 0)
    def _():
        clear(leaves.at[1:3, 0])

    @pl.when(d == nd - 1)
    def _():
        clear(leaves.at[1:3, 3])

    clear(trs)
    for k in range(16):
        trs[2 * k : 2 * k + 2, 0:nq] = tr_ref[k]
    loads[0].wait()
    loads[2].start()
    loads[3].start()
    for i in range(2):
        for j in range(2):
            live = live_ref[i, j].astype(f32)
            for c in range(2):
                leaves[1 + i, 1 + j, c] = (raw[c, i, j].astype(f32) * live).astype(bf16)

    loads[1].wait()
    rows = min(256, total_dirs)
    for rc in range(2):
        cols = slice(rc * LANES, (rc + 1) * LANES)

        @pl.loop(0, total_dirs // rows)
        def _(n, rc=rc, cols=cols):
            right = stacked(
                *[
                    jnp.concatenate([leaves[1 + i, 1 + j, c, :, cols] for i in range(2) for j in range(2)], axis=0)
                    for c in range(2)
                ]
            )
            some = pl.ds(pl.multiple_of(n * rows, rows), rows)
            left = jnp.concatenate(
                [agg[c, i, j, some] for c in range(2) for i in range(2) for j in range(2)], axis=1
            )
            both = dot(left, right)
            for c in range(2):
                pat[rc, pl.ds(n * (rows // nq), rows // nq), c] = (
                    both[:, c * LANES : (c + 1) * LANES].astype(bf16).reshape(rows // nq, nq, LANES)
                )

    pl.semaphore_wait(bar, owners - 1 + 2 + jnp.where(s != z, 1, 0))

    def remote(src, dst, sems, i, device):
        return pltpu.make_async_remote_copy(
            src_ref=src, dst_ref=dst, send_sem=sems.at[0, i], recv_sem=sems.at[1, i],
            device_id=device, device_id_type=MESH,
        )

    swap = remote(trs, trd, t_sem, 0, (z, s * nx + x))

    @pl.when(s != z)
    def _():
        swap.start()

    @pl.when(s == z)
    def _():
        trd[...] = trs[...]

    left_end, right_end = x == 0, x == nx - 1
    before, after = z > 0, z < nz - 1
    left = (s, z * nx + jnp.where(left_end, nx - 1, x - 1))
    right = (s, z * nx + jnp.where(right_end, 0, x + 1))
    prev, nxt = (s, d - nx), (s, d + nx)

    def to_left(r, src=None):
        return remote(leaves.at[1 + r, 1] if src is None else src, leaves.at[1 + r, 3], nx_sem, r, left)

    def to_right(r, src=None):
        return remote(leaves.at[1 + r, 2] if src is None else src, leaves.at[1 + r, 0], nx_sem, 2 + r, right)

    first_left = remote(leaves.at[1, 1], hop.at[0], hop_sem, 0, prev)
    first_right = remote(leaves.at[1, 2], hop.at[0], hop_sem, 0, nxt)
    second_left = remote(leaves.at[2, 1], hop.at[1], hop_sem, 1, left)
    second_right = remote(leaves.at[2, 2], hop.at[1], hop_sem, 1, right)

    def pass_on(column, recv, device):
        return pltpu.make_async_remote_copy(
            src_ref=hop.at[1], dst_ref=leaves.at[2, column], send_sem=hop_sem.at[0, 2], recv_sem=nx_sem.at[1, recv],
            device_id=device, device_id_type=MESH,
        )


    spans = ((1, 3), (0, 1), (3, 4))
    up = [
        remote(leaves.at[1, a:b], leaves.at[3, a:b], ny_sem, i, (s - 1, d)) for i, (a, b) in enumerate(spans)
    ]
    down = [
        remote(leaves.at[2, a:b], leaves.at[0, a:b], ny_sem, 3 + i, (s + 1, d)) for i, (a, b) in enumerate(spans)
    ]

    def start_columns():
        for r in range(2):

            @pl.when(jnp.logical_not(left_end))
            def _(r=r):
                to_left(r).start()

            @pl.when(jnp.logical_not(right_end))
            def _(r=r):
                to_right(r).start()

        @pl.when(left_end & before)
        def _():
            second_left.start()

        @pl.when(right_end & after)
        def _():
            second_right.start()

    def start_hops():
        @pl.when(left_end & before)
        def _():
            first_left.start()

        @pl.when(right_end & after)
        def _():
            first_right.start()

    def pass_first():
        @pl.when(left_end & after)
        def _():
            first_left.wait_recv()
            to_left(0, hop.at[0]).start()

        @pl.when(right_end & before)
        def _():
            first_right.wait_recv()
            to_right(0, hop.at[0]).start()

    def pass_second():
        @pl.when(right_end & before)
        def _():
            second_left.wait_recv()
            pass_on(3, 1, prev).start()

        @pl.when(left_end & after)
        def _():
            second_right.wait_recv()
            pass_on(0, 3, nxt).start()

    def columns_came(r):
        @pl.when(d < nd - 1)
        def _():
            to_left(r).wait_recv()

        @pl.when(d > 0)
        def _():
            to_right(r).wait_recv()

    def start_up(which):
        @pl.when(s > 0)
        def _():
            for i in which:
                up[i].start()

    def start_down(which):
        @pl.when(s < ns - 1)
        def _():
            for i in which:
                down[i].start()

    start_hops()

    @pl.loop(0, 2)
    def _(rc):
        dst, arrived = grid.at[rc, 2 + s, 2 + x], r1_sem.at[rc, x // 2, y]
        for y_step in y_order:
            for n, other in enumerate(cores):
                row = 2 * lax.rem(y + y_step, ny) + other
                for x_step, col in zip(x_order, columns):
                    if y_step or x_step or n == 0:
                        send(pat.at[rc, row * nx + col], dst, row, col, s1_sem.at[rc], arrived)
        pltpu.make_async_copy(pat.at[rc, me], dst, arrived).start()

    start_columns()
    start_up((0,))
    start_down((0,))
    for rc in range(2):
        clear(grid.at[rc, 0:2])
        clear(grid.at[rc, ns + 2 : ns + 4])

    @pl.when(z == 0)
    def _():
        for rc in range(2):
            clear(grid.at[rc, 2 : ns + 2, 0:2])

    @pl.when(z == nz - 1)
    def _():
        for rc in range(2):
            clear(grid.at[rc, 2 : ns + 2, nx + 2 : nx + 4])

    def near(p, q):
        targets = [(i, j) for i in range(2) for j in range(2) if 0 <= p - i <= 2 and 0 <= q - j <= 2]
        right = stacked(leaves[p, q, 0], leaves[p, q, 1])
        left = jnp.concatenate(
            [
                jnp.concatenate([nb[c, i, j, 3 * (p - i) + q - j] for c in range(2)], axis=1)
                for i, j in targets
            ],
            axis=0,
        )
        both = dot(left, right)
        rows = left.shape[0] // len(targets)
        width = both.shape[1] // 2
        for n, (i, j) in enumerate(targets):
            for c in range(2):
                part = both[n * rows : (n + 1) * rows, c * width : (c + 1) * width]
                part = part * live_ref[i, j].astype(f32)
                acc[c, i, j] = part if (p, q) == (1, 1) else acc[c, i, j] + part

    loads[2].wait()

    for p in range(1, 3):
        for q in range(1, 3):
            near(p, q)

    def plane(rc, side, first, count):
        rows = pl.ds(2 + first, count)
        own = grid.at[rc, rows, 2:4] if side == 0 else grid.at[rc, rows, nx : nx + 2]
        there = grid.at[rc, rows, nx + 2 : nx + 4] if side == 0 else grid.at[rc, rows, 0:2]
        return pltpu.make_async_remote_copy(
            src_ref=own, dst_ref=there, send_sem=sz_sem.at[rc, side], recv_sem=rz_sem.at[rc, side],
            device_id=(s, d - nx if side == 0 else d + nx), device_id_type=MESH,
        )

    for rc in range(2):
        @pl.loop(0, ny)
        def _(i, rc=rc):
            from_y = y_at(i)
            for side in range(2):
                part = grid.at[rc, pl.ds(2 + 2 * from_y, 2), 2 + 2 * side : 4 + 2 * side]
                pltpu.make_async_copy(part, part, r1_sem.at[rc, side, from_y]).wait()

                @pl.when(z > 0 if side == 0 else z < nz - 1)
                def _(rc=rc, side=side, from_y=from_y):
                    plane(rc, side, 2 * from_y, 2).start()

        if rc == 0:
            pass_first()
            @pl.when(s != z)
            def _():
                swap.wait_recv()

            turned = trd[...].T
            half, wide = mix.shape[1] // 2, mix.shape[2]
            lane = lax.broadcasted_iota(jnp.int32, (nq, wide), 1)
            same = lax.rem(lane, nq) == lax.broadcasted_iota(jnp.int32, (nq, wide), 0)
            imag = lax.rem(lane // nq, 2) == 1
            source = jnp.where(same, lane // (2 * nq), -1)
            for row_step in range(-2, 3):
                ks = [(k, b) for k, (a, b) in enumerate(far_offsets) if a == row_step]
                for c in range(2):
                    rows = [jnp.zeros((nq, wide), f32) for _ in range(nx)]
                    for k, b in ks:
                        p, q = (jnp.broadcast_to(turned[0:nq, 2 * k + n : 2 * k + n + 1], (nq, wide)) for n in range(2))
                        value = jnp.where(imag, p, q) if c else jnp.where(imag, -q, p)
                        rows = [jnp.where(source == 2 + col + b, value, rows[col]) for col in range(nx)]
                    for col in range(nx):
                        first = (2 * col + c) * nq
                        high = rows[col].astype(bf16)
                        mix[row_step + 2, first : first + nq] = high
                        rest = (rows[col] - high.astype(f32)).astype(bf16)
                        mix[row_step + 2, half + first : half + first + nq] = rest

    for rc in range(2):

        @pl.when(z < nz - 1)
        def _(rc=rc):
            plane(rc, 0, 0, ns).wait_recv()

        @pl.when(z > 0)
        def _(rc=rc):
            plane(rc, 1, 0, ns).wait_recv()

        @pl.loop(0, ny)
        def _(i, rc=rc):
            first = 2 * y_at(i)
            total = jnp.zeros((2 * nx * nq, 2 * LANES), f32)
            for row_step in range(5):
                right = jnp.concatenate(
                    [grid[rc, first + n + row_step].reshape(2 * (nx + 4) * nq, LANES) for n in range(2)], axis=1
                )
                term = dot(mix[row_step], right)
                total += (term[: 2 * nx * nq] + term[2 * nx * nq :]).astype(bf16).astype(f32)
            for n in range(2):
                inc[rc, pl.ds((first + n) * nx, nx)] = (
                    total[:, n * LANES : (n + 1) * LANES].astype(bf16).reshape(nx, 2, nq, LANES)
                )
            dst = back.at[rc, me]
            for n, other in enumerate(cores):
                row = first + other
                for x_step, col in zip(x_order, columns):
                    src, sems = inc.at[rc, row * nx + col], (s2_sem.at[rc], r2_sem.at[rc])
                    if n == 0 or x_step:
                        send(src, dst, row, col, *sems)
                        continue

                    @pl.when(i < ny - 1)
                    def _(src=src, row=row, col=col, sems=sems):
                        send(src, dst, row, col, *sems)

                    @pl.when(i == ny - 1)
                    def _(src=src, sems=sems):
                        pltpu.make_async_copy(src, dst, sems[1]).start()

        if rc == 0:
            pass_second()
            columns_came(0)
            start_up((1, 2))
        else:
            columns_came(1)
            start_down((1, 2))

    for p in range(1, 3):
        for q in (0, 3):
            near(p, q)

    loads[3].wait()

    def far(rc):
        cols = slice(rc * LANES, (rc + 1) * LANES)
        whole = back.at[rc]
        pltpu.make_async_copy(whole, whole, r2_sem.at[rc]).wait()
        right = stacked(*[back[rc, :, c].reshape(owners * nq, LANES) for c in range(2)])
        for i in range(2):
            left = jnp.concatenate(
                [jnp.concatenate([dis[c, i, j] for c in range(2)], axis=1) for j in range(2)], axis=0
            )
            both = dot(left, right)
            rows = left.shape[0] // 2
            for j in range(2):
                live = live_ref[i, j].astype(f32)
                for c in range(2):
                    part = both[j * rows : (j + 1) * rows, c * LANES : (c + 1) * LANES]
                    acc[c, i, j, :, cols] += part * live

    far(0)

    @pl.when(s < ns - 1)
    def _():
        for copy in up:
            copy.wait_recv()

    for q in range(4):
        near(3, q)

    @pl.when(s > 0)
    def _():
        for copy in down:
            copy.wait_recv()

    for q in range(4):
        near(0, q)

    far(1)

    @pl.when(s != z)
    def _():
        swap.wait_send()

    @pl.when(jnp.logical_not(left_end) | after)
    def _():
        to_left(0).wait_send()

    @pl.when(jnp.logical_not(right_end) | before)
    def _():
        to_right(0).wait_send()

    @pl.when(jnp.logical_not(left_end))
    def _():
        to_left(1).wait_send()

    @pl.when(jnp.logical_not(right_end))
    def _():
        to_right(1).wait_send()

    @pl.when(left_end & before | right_end & after)
    def _():
        first_left.wait_send()
        second_left.wait_send()

    @pl.when(right_end & before | left_end & after)
    def _():
        pass_on(3, 1, prev).wait_send()

    @pl.when(s > 0)
    def _():
        for copy in up:
            copy.wait_send()

    @pl.when(s < ns - 1)
    def _():
        for copy in down:
            copy.wait_send()

    for rc in range(2):
        sent = inc.at[rc, 0 : owners - 1]
        pltpu.make_async_copy(sent, sent, s1_sem.at[rc]).wait()
        pltpu.make_async_copy(sent, sent, s2_sem.at[rc]).wait()

        @pl.when(z > 0)
        def _(rc=rc):
            plane(rc, 0, 0, ns).wait_send()

        @pl.when(z < nz - 1)
        def _(rc=rc):
            plane(rc, 1, 0, ns).wait_send()


def shards(ns, nd, unknowns, leaf_live, near_blocks, aggregate, disaggregate, translate):
    nq = translate.shape[2]
    leaf, sides = unknowns.shape[3:]
    dirs = aggregate.shape[3]
    bf16, f32 = jnp.bfloat16, jnp.float32
    owners = ns * PLANE_COLS
    any_space = pl.BlockSpec(memory_space=pl.ANY)
    dma = pltpu.SemaphoreType.DMA
    field = pl.pallas_call(
        functools.partial(kernel, ns, nd),
        out_shape=pltpu.VMEM(unknowns.shape, f32),
        in_specs=[
            pl.BlockSpec(memory_space=pltpu.SMEM),
            any_space,
            any_space,
            any_space,
            any_space,
            pl.BlockSpec(memory_space=pltpu.VMEM),
        ],
        out_specs=pl.BlockSpec(memory_space=pltpu.VMEM),
        scratch_shapes=[
            pltpu.VMEM(unknowns.shape, bf16),
            pltpu.VMEM((4, 4, 2, leaf, sides), bf16),
            pltpu.VMEM((2, 2, leaf, sides), bf16),
            pltpu.VMEM(near_blocks.shape, bf16),
            pltpu.VMEM(aggregate.shape, bf16),
            pltpu.VMEM(disaggregate.shape, bf16),
            pltpu.VMEM((2, owners, 2, nq, LANES), bf16),
            pltpu.VMEM((2, ns + 4, PLANE_COLS + 4, 2, nq, LANES), bf16),
            pltpu.VMEM((2, owners, 2, nq, LANES), bf16),
            pltpu.VMEM((2, owners, 2, nq, LANES), bf16),
            pltpu.VMEM((32, LANES), f32),
            pltpu.VMEM((32, LANES), f32),
            pltpu.VMEM((5, 4 * PLANE_COLS * nq, 2 * (PLANE_COLS + 4) * nq), bf16),
            dma((4,)),
            dma((2, 3)),
            dma((2, 4)),
            dma((2, 6)),
            dma((2, 1)),
            dma((2,)),
            dma((2, 2, ns // 2)),
            dma((2, 2)),
            dma((2, 2)),
            dma((2,)),
            dma((2,)),
        ],
        compiler_params=pltpu.CompilerParams(
            collective_id=0, has_side_effects=True, vmem_limit_bytes=56 * 1024 * 1024
        ),
    )(leaf_live, unknowns, near_blocks, aggregate, disaggregate, translate)
    return field


def solution(mesh):
    in_specs = (
        P(None, "sect", "dir", None, None),
        P("sect", "dir"),
        P(None, "sect", "dir", None, None, None),
        P(None, "sect", "dir", None, None),
        P(None, "sect", "dir", None, None),
        P(None, None, "dir"),
    )
    out_specs = P(None, "sect", "dir", None, None)
    body = functools.partial(shards, mesh.shape["sect"], mesh.shape["dir"])
    return jax.shard_map(body, mesh=mesh, in_specs=in_specs, out_specs=out_specs, check_vma=False)
```

```python
import functools

import jax
import jax.numpy as jnp
from jax import lax
from jax.experimental import pallas as pl
from jax.experimental.pallas import tpu as pltpu
from jax.sharding import PartitionSpec as P

MESH = pl.DeviceIdType.MESH
PLANE_COLS = 4
LANES = 128

far_offsets = [(a, b) for a in range(-2, 3) for b in range(-2, 3) if max(abs(a), abs(b)) == 2]


def stacked(real, imag, axis=0):
    top = jnp.concatenate([real, imag], axis=1)
    low = jnp.concatenate([-imag, real], axis=1)
    return jnp.concatenate([top, low], axis=0)


def dot(left, right):
    return jnp.dot(left, right, preferred_element_type=jnp.float32)


def kernel(
    ns, nd, live_ref, unk_hbm, nb_hbm, agg_hbm, dis_hbm, tr_ref, acc,
    raw, leaves, hop, nb, agg, dis, pat, grid, inc, back, trs, trd, mix,
    load_sem, hop_sem, nx_sem, ny_sem, t_sem, s1_sem, r1_sem, sz_sem, rz_sem, s2_sem, r2_sem,
):
    nx = PLANE_COLS
    nz = nd // nx
    owners = ns * nx
    total_dirs = agg.shape[3]
    nq = total_dirs // owners
    f32, bf16 = jnp.float32, jnp.bfloat16

    s, d = lax.axis_index("sect"), lax.axis_index("dir")
    z, x = d // nx, lax.rem(d, nx)
    me = s * nx + x

    loads = [
        pltpu.make_async_copy(src, dst, load_sem.at[i])
        for i, (src, dst) in enumerate(((unk_hbm, raw), (agg_hbm, agg), (nb_hbm, nb), (dis_hbm, dis)))
    ]
    loads[0].start()
    loads[1].start()

    ny = ns // 2
    y, core = s // 2, lax.rem(s, 2)
    y_order = sorted(range(ny), key=lambda step: (-min(step, ny - step), step))
    x_order = sorted(range(nx), key=lambda step: (-min(step, nx - step), step))
    y_digits = sum(step * 4**i for i, step in enumerate(y_order))
    cores = (1 - core, core)

    def y_at(i):
        return lax.rem(y + lax.rem(lax.shift_right_logical(jnp.int32(y_digits), 2 * i), 4), ny)

    columns = [lax.rem(x + step, nx) for step in x_order]

    def send(src, dst, row, col, send_sem, recv_sem):
        pltpu.make_async_remote_copy(
            src_ref=src, dst_ref=dst, send_sem=send_sem, recv_sem=recv_sem,
            device_id=(row, z * nx + col), device_id_type=MESH,
        ).start()

    bar = pltpu.get_barrier_semaphore()

    def greet(device):
        pl.semaphore_signal(bar, inc=1, device_id=device, device_id_type=MESH)

    @pl.when(s != z)
    def _():
        greet((z, s * nx + x))

    for step in (1, nz - 1):
        greet((s, lax.rem(z + step, nz) * nx + x))

    def hops(step):
        return min(step[0], ny - step[0]) + min(step[2], nx - step[2])

    steps = [(a, b, c) for a in range(ny) for b in range(2) for c in range(nx)][1:]
    for a, b, c in sorted(steps, key=lambda step: -hops(step)):
        greet((lax.rem(y + a, ny) * 2 + lax.rem(core + b, 2), z * nx + lax.rem(x + c, nx)))

    def clear(ref):
        ref[...] = jnp.zeros(ref.shape, ref.dtype)

    @pl.when(s == 0)
    def _():
        clear(leaves.at[0])

    @pl.when(s == ns - 1)
    def _():
        clear(leaves.at[3])

    @pl.when(d == 0)
    def _():
        clear(leaves.at[1:3, 0])

    @pl.when(d == nd - 1)
    def _():
        clear(leaves.at[1:3, 3])

    clear(trs)
    for k in range(16):
        trs[2 * k : 2 * k + 2, 0:nq] = tr_ref[k]
    loads[0].wait()
    loads[2].start()
    loads[3].start()
    for i in range(2):
        for j in range(2):
            live = live_ref[i, j].astype(f32)
            for c in range(2):
                leaves[1 + i, 1 + j, c] = (raw[c, i, j].astype(f32) * live).astype(bf16)

    loads[1].wait()
    rows = min(256, total_dirs)
    for rc in range(2):
        cols = slice(rc * LANES, (rc + 1) * LANES)

        @pl.loop(0, total_dirs // rows)
        def _(n, rc=rc, cols=cols):
            right = stacked(
                *[
                    jnp.concatenate([leaves[1 + i, 1 + j, c, :, cols] for i in range(2) for j in range(2)], axis=0)
                    for c in range(2)
                ]
            )
            some = pl.ds(pl.multiple_of(n * rows, rows), rows)
            left = jnp.concatenate(
                [agg[c, i, j, some] for c in range(2) for i in range(2) for j in range(2)], axis=1
            )
            both = dot(left, right)
            for c in range(2):
                pat[rc, pl.ds(n * (rows // nq), rows // nq), c] = (
                    both[:, c * LANES : (c + 1) * LANES].astype(bf16).reshape(rows // nq, nq, LANES)
                )

    pl.semaphore_wait(bar, owners - 1 + 2 + jnp.where(s != z, 1, 0))

    def remote(src, dst, sems, i, device):
        return pltpu.make_async_remote_copy(
            src_ref=src, dst_ref=dst, send_sem=sems.at[0, i], recv_sem=sems.at[1, i],
            device_id=device, device_id_type=MESH,
        )

    swap = remote(trs, trd, t_sem, 0, (z, s * nx + x))

    left_end, right_end = x == 0, x == nx - 1
    before, after = z > 0, z < nz - 1
    left = (s, z * nx + jnp.where(left_end, nx - 1, x - 1))
    right = (s, z * nx + jnp.where(right_end, 0, x + 1))
    prev, nxt = (s, d - nx), (s, d + nx)

    def to_left(r, src=None):
        return remote(leaves.at[1 + r, 1] if src is None else src, leaves.at[1 + r, 3], nx_sem, r, left)

    def to_right(r, src=None):
        return remote(leaves.at[1 + r, 2] if src is None else src, leaves.at[1 + r, 0], nx_sem, 2 + r, right)

    first_left = remote(leaves.at[1, 1], hop.at[0], hop_sem, 0, prev)
    first_right = remote(leaves.at[1, 2], hop.at[0], hop_sem, 0, nxt)
    second_left = remote(leaves.at[2, 1], hop.at[1], hop_sem, 1, left)
    second_right = remote(leaves.at[2, 2], hop.at[1], hop_sem, 1, right)

    def pass_on(column, recv, device):
        return pltpu.make_async_remote_copy(
            src_ref=hop.at[1], dst_ref=leaves.at[2, column], send_sem=hop_sem.at[0, 2], recv_sem=nx_sem.at[1, recv],
            device_id=device, device_id_type=MESH,
        )


    spans = ((1, 3), (0, 1), (3, 4))
    up = [
        remote(leaves.at[1, a:b], leaves.at[3, a:b], ny_sem, i, (s - 1, d)) for i, (a, b) in enumerate(spans)
    ]
    down = [
        remote(leaves.at[2, a:b], leaves.at[0, a:b], ny_sem, 3 + i, (s + 1, d)) for i, (a, b) in enumerate(spans)
    ]

    def start_columns():
        for r in range(2):

            @pl.when(jnp.logical_not(left_end))
            def _(r=r):
                to_left(r).start()

            @pl.when(jnp.logical_not(right_end))
            def _(r=r):
                to_right(r).start()

        @pl.when(left_end & before)
        def _():
            second_left.start()

        @pl.when(right_end & after)
        def _():
            second_right.start()

    def start_hops():
        @pl.when(left_end & before)
        def _():
            first_left.start()

        @pl.when(right_end & after)
        def _():
            first_right.start()

    def pass_first():
        @pl.when(left_end & after)
        def _():
            first_left.wait_recv()
            to_left(0, hop.at[0]).start()

        @pl.when(right_end & before)
        def _():
            first_right.wait_recv()
            to_right(0, hop.at[0]).start()

    def pass_second():
        @pl.when(right_end & before)
        def _():
            second_left.wait_recv()
            pass_on(3, 1, prev).start()

        @pl.when(left_end & after)
        def _():
            second_right.wait_recv()
            pass_on(0, 3, nxt).start()

    def columns_came(r):
        @pl.when(d < nd - 1)
        def _():
            to_left(r).wait_recv()

        @pl.when(d > 0)
        def _():
            to_right(r).wait_recv()

    def start_up(which):
        @pl.when(s > 0)
        def _():
            for i in which:
                up[i].start()

    def start_down(which):
        @pl.when(s < ns - 1)
        def _():
            for i in which:
                down[i].start()

    start_hops()

    @pl.loop(0, 2)
    def _(rc):
        dst, arrived = grid.at[rc, 2 + s, 2 + x], r1_sem.at[rc, x // 2, y]
        for y_step in y_order:
            for other in range(2):
                row = 2 * lax.rem(y + y_step, ny) + other
                for x_step, col in zip(x_order, columns):
                    if y_step or x_step:
                        send(pat.at[rc, row * nx + col], dst, row, col, s1_sem.at[rc], arrived)
                        continue

                    @pl.when(core != other)
                    def _(row=row, col=col):
                        send(pat.at[rc, row * nx + col], dst, row, col, s1_sem.at[rc], arrived)

        pltpu.make_async_copy(pat.at[rc, me], dst, arrived).start()

    @pl.when(s != z)
    def _():
        swap.start()

    @pl.when(s == z)
    def _():
        trd[...] = trs[...]

    start_columns()
    start_up((0,))
    start_down((0,))
    for rc in range(2):
        clear(grid.at[rc, 0:2])
        clear(grid.at[rc, ns + 2 : ns + 4])

    @pl.when(z == 0)
    def _():
        for rc in range(2):
            clear(grid.at[rc, 2 : ns + 2, 0:2])

    @pl.when(z == nz - 1)
    def _():
        for rc in range(2):
            clear(grid.at[rc, 2 : ns + 2, nx + 2 : nx + 4])

    def near(p, q):
        targets = [(i, j) for i in range(2) for j in range(2) if 0 <= p - i <= 2 and 0 <= q - j <= 2]
        right = stacked(leaves[p, q, 0], leaves[p, q, 1])
        left = jnp.concatenate(
            [
                jnp.concatenate([nb[c, i, j, 3 * (p - i) + q - j] for c in range(2)], axis=1)
                for i, j in targets
            ],
            axis=0,
        )
        both = dot(left, right)
        rows = left.shape[0] // len(targets)
        width = both.shape[1] // 2
        for n, (i, j) in enumerate(targets):
            for c in range(2):
                part = both[n * rows : (n + 1) * rows, c * width : (c + 1) * width]
                part = part * live_ref[i, j].astype(f32)
                acc[c, i, j] = part if (p, q) == (1, 1) else acc[c, i, j] + part

    loads[2].wait()

    for p in range(1, 3):
        for q in range(1, 3):
            near(p, q)

    def plane(rc, side, first, count):
        rows = pl.ds(2 + first, count)
        own = grid.at[rc, rows, 2:4] if side == 0 else grid.at[rc, rows, nx : nx + 2]
        there = grid.at[rc, rows, nx + 2 : nx + 4] if side == 0 else grid.at[rc, rows, 0:2]
        return pltpu.make_async_remote_copy(
            src_ref=own, dst_ref=there, send_sem=sz_sem.at[rc, side], recv_sem=rz_sem.at[rc, side],
            device_id=(s, d - nx if side == 0 else d + nx), device_id_type=MESH,
        )

    for rc in range(2):
        @pl.loop(0, ny)
        def _(i, rc=rc):
            from_y = y_at(i)
            for side in range(2):
                part = grid.at[rc, pl.ds(2 + 2 * from_y, 2), 2 + 2 * side : 4 + 2 * side]
                pltpu.make_async_copy(part, part, r1_sem.at[rc, side, from_y]).wait()

                @pl.when(z > 0 if side == 0 else z < nz - 1)
                def _(rc=rc, side=side, from_y=from_y):
                    plane(rc, side, 2 * from_y, 2).start()

        if rc == 0:
            pass_first()
            @pl.when(s != z)
            def _():
                swap.wait_recv()

            turned = trd[...].T
            half, wide = mix.shape[1] // 2, mix.shape[2]
            lane = lax.broadcasted_iota(jnp.int32, (nq, wide), 1)
            same = lax.rem(lane, nq) == lax.broadcasted_iota(jnp.int32, (nq, wide), 0)
            imag = lax.rem(lane // nq, 2) == 1
            source = jnp.where(same, lane // (2 * nq), -1)
            for row_step in range(-2, 3):
                ks = [(k, b) for k, (a, b) in enumerate(far_offsets) if a == row_step]
                for c in range(2):
                    rows = [jnp.zeros((nq, wide), f32) for _ in range(nx)]
                    for k, b in ks:
                        p, q = (jnp.broadcast_to(turned[0:nq, 2 * k + n : 2 * k + n + 1], (nq, wide)) for n in range(2))
                        value = jnp.where(imag, p, q) if c else jnp.where(imag, -q, p)
                        rows = [jnp.where(source == 2 + col + b, value, rows[col]) for col in range(nx)]
                    for col in range(nx):
                        first = (2 * col + c) * nq
                        high = rows[col].astype(bf16)
                        mix[row_step + 2, first : first + nq] = high
                        rest = (rows[col] - high.astype(f32)).astype(bf16)
                        mix[row_step + 2, half + first : half + first + nq] = rest

    for rc in range(2):

        @pl.when(z < nz - 1)
        def _(rc=rc):
            plane(rc, 0, 0, ns).wait_recv()

        @pl.when(z > 0)
        def _(rc=rc):
            plane(rc, 1, 0, ns).wait_recv()

        @pl.loop(0, ny)
        def _(i, rc=rc):
            first = 2 * y_at(i)
            total = jnp.zeros((2 * nx * nq, 2 * LANES), f32)
            for row_step in range(5):
                right = jnp.concatenate(
                    [grid[rc, first + n + row_step].reshape(2 * (nx + 4) * nq, LANES) for n in range(2)], axis=1
                )
                term = dot(mix[row_step], right)
                total += (term[: 2 * nx * nq] + term[2 * nx * nq :]).astype(bf16).astype(f32)
            for n in range(2):
                inc[rc, pl.ds((first + n) * nx, nx)] = (
                    total[:, n * LANES : (n + 1) * LANES].astype(bf16).reshape(nx, 2, nq, LANES)
                )
            dst = back.at[rc, me]
            for n, other in enumerate(cores):
                row = first + other
                for x_step, col in zip(x_order, columns):
                    src, sems = inc.at[rc, row * nx + col], (s2_sem.at[rc], r2_sem.at[rc])
                    if n == 0 or x_step:
                        send(src, dst, row, col, *sems)
                        continue

                    @pl.when(i < ny - 1)
                    def _(src=src, row=row, col=col, sems=sems):
                        send(src, dst, row, col, *sems)

                    @pl.when(i == ny - 1)
                    def _(src=src, sems=sems):
                        pltpu.make_async_copy(src, dst, sems[1]).start()

        if rc == 0:
            pass_second()
            columns_came(0)
            start_up((1, 2))
        else:
            columns_came(1)
            start_down((1, 2))

    for p in range(1, 3):
        for q in (0, 3):
            near(p, q)

    loads[3].wait()

    def far(rc):
        cols = slice(rc * LANES, (rc + 1) * LANES)
        whole = back.at[rc]
        pltpu.make_async_copy(whole, whole, r2_sem.at[rc]).wait()
        right = stacked(*[back[rc, :, c].reshape(owners * nq, LANES) for c in range(2)])
        for i in range(2):
            left = jnp.concatenate(
                [jnp.concatenate([dis[c, i, j] for c in range(2)], axis=1) for j in range(2)], axis=0
            )
            both = dot(left, right)
            rows = left.shape[0] // 2
            for j in range(2):
                live = live_ref[i, j].astype(f32)
                for c in range(2):
                    part = both[j * rows : (j + 1) * rows, c * LANES : (c + 1) * LANES]
                    acc[c, i, j, :, cols] += part * live

    far(0)

    @pl.when(s < ns - 1)
    def _():
        for copy in up:
            copy.wait_recv()

    for q in range(4):
        near(3, q)

    @pl.when(s > 0)
    def _():
        for copy in down:
            copy.wait_recv()

    for q in range(4):
        near(0, q)

    far(1)

    @pl.when(s != z)
    def _():
        swap.wait_send()

    @pl.when(jnp.logical_not(left_end) | after)
    def _():
        to_left(0).wait_send()

    @pl.when(jnp.logical_not(right_end) | before)
    def _():
        to_right(0).wait_send()

    @pl.when(jnp.logical_not(left_end))
    def _():
        to_left(1).wait_send()

    @pl.when(jnp.logical_not(right_end))
    def _():
        to_right(1).wait_send()

    @pl.when(left_end & before | right_end & after)
    def _():
        first_left.wait_send()
        second_left.wait_send()

    @pl.when(right_end & before | left_end & after)
    def _():
        pass_on(3, 1, prev).wait_send()

    @pl.when(s > 0)
    def _():
        for copy in up:
            copy.wait_send()

    @pl.when(s < ns - 1)
    def _():
        for copy in down:
            copy.wait_send()

    for rc in range(2):
        sent = inc.at[rc, 0 : owners - 1]
        pltpu.make_async_copy(sent, sent, s1_sem.at[rc]).wait()
        pltpu.make_async_copy(sent, sent, s2_sem.at[rc]).wait()

        @pl.when(z > 0)
        def _(rc=rc):
            plane(rc, 0, 0, ns).wait_send()

        @pl.when(z < nz - 1)
        def _(rc=rc):
            plane(rc, 1, 0, ns).wait_send()


def shards(ns, nd, unknowns, leaf_live, near_blocks, aggregate, disaggregate, translate):
    nq = translate.shape[2]
    leaf, sides = unknowns.shape[3:]
    dirs = aggregate.shape[3]
    bf16, f32 = jnp.bfloat16, jnp.float32
    owners = ns * PLANE_COLS
    any_space = pl.BlockSpec(memory_space=pl.ANY)
    dma = pltpu.SemaphoreType.DMA
    field = pl.pallas_call(
        functools.partial(kernel, ns, nd),
        out_shape=pltpu.VMEM(unknowns.shape, f32),
        in_specs=[
            pl.BlockSpec(memory_space=pltpu.SMEM),
            any_space,
            any_space,
            any_space,
            any_space,
            pl.BlockSpec(memory_space=pltpu.VMEM),
        ],
        out_specs=pl.BlockSpec(memory_space=pltpu.VMEM),
        scratch_shapes=[
            pltpu.VMEM(unknowns.shape, bf16),
            pltpu.VMEM((4, 4, 2, leaf, sides), bf16),
            pltpu.VMEM((2, 2, leaf, sides), bf16),
            pltpu.VMEM(near_blocks.shape, bf16),
            pltpu.VMEM(aggregate.shape, bf16),
            pltpu.VMEM(disaggregate.shape, bf16),
            pltpu.VMEM((2, owners, 2, nq, LANES), bf16),
            pltpu.VMEM((2, ns + 4, PLANE_COLS + 4, 2, nq, LANES), bf16),
            pltpu.VMEM((2, owners, 2, nq, LANES), bf16),
            pltpu.VMEM((2, owners, 2, nq, LANES), bf16),
            pltpu.VMEM((32, LANES), f32),
            pltpu.VMEM((32, LANES), f32),
            pltpu.VMEM((5, 4 * PLANE_COLS * nq, 2 * (PLANE_COLS + 4) * nq), bf16),
            dma((4,)),
            dma((2, 3)),
            dma((2, 4)),
            dma((2, 6)),
            dma((2, 1)),
            dma((2,)),
            dma((2, 2, ns // 2)),
            dma((2, 2)),
            dma((2, 2)),
            dma((2,)),
            dma((2,)),
        ],
        compiler_params=pltpu.CompilerParams(
            collective_id=0, has_side_effects=True, vmem_limit_bytes=56 * 1024 * 1024
        ),
    )(leaf_live, unknowns, near_blocks, aggregate, disaggregate, translate)
    return field


def solution(mesh):
    in_specs = (
        P(None, "sect", "dir", None, None),
        P("sect", "dir"),
        P(None, "sect", "dir", None, None, None),
        P(None, "sect", "dir", None, None),
        P(None, "sect", "dir", None, None),
        P(None, None, "dir"),
    )
    out_specs = P(None, "sect", "dir", None, None)
    body = functools.partial(shards, mesh.shape["sect"], mesh.shape["dir"])
    return jax.shard_map(body, mesh=mesh, in_specs=in_specs, out_specs=out_specs, check_vma=False)
```

```python
import functools

import jax
import jax.numpy as jnp
from jax import lax
from jax.experimental import pallas as pl
from jax.experimental.pallas import tpu as pltpu
from jax.sharding import PartitionSpec as P

MESH = pl.DeviceIdType.MESH
PLANE_COLS = 4
LANES = 128

far_offsets = [(a, b) for a in range(-2, 3) for b in range(-2, 3) if max(abs(a), abs(b)) == 2]


def stacked(real, imag, axis=0):
    top = jnp.concatenate([real, imag], axis=1)
    low = jnp.concatenate([-imag, real], axis=1)
    return jnp.concatenate([top, low], axis=0)


def dot(left, right):
    return jnp.dot(left, right, preferred_element_type=jnp.float32)


def kernel(
    ns, nd, live_ref, unk_hbm, nb_hbm, agg_hbm, dis_hbm, tr_ref, acc,
    raw, leaves, hop, nb, agg, dis, pat, grid, inc, back, trs, trd, mix,
    load_sem, hop_sem, nx_sem, ny_sem, t_sem, s1_sem, r1_sem, sz_sem, rz_sem, s2_sem, r2_sem,
):
    nx = PLANE_COLS
    nz = nd // nx
    owners = ns * nx
    total_dirs = agg.shape[3]
    nq = total_dirs // owners
    f32, bf16 = jnp.float32, jnp.bfloat16

    s, d = lax.axis_index("sect"), lax.axis_index("dir")
    z, x = d // nx, lax.rem(d, nx)
    me = s * nx + x

    loads = [
        pltpu.make_async_copy(src, dst, load_sem.at[i])
        for i, (src, dst) in enumerate(((unk_hbm, raw), (agg_hbm, agg), (nb_hbm, nb), (dis_hbm, dis)))
    ]
    loads[0].start()
    loads[1].start()

    ny = ns // 2
    y, core = s // 2, lax.rem(s, 2)
    y_order = sorted(range(ny), key=lambda step: (-min(step, ny - step), step))
    x_order = sorted(range(nx), key=lambda step: (-min(step, nx - step), step))
    y_digits = sum(step * 4**i for i, step in enumerate(y_order))
    cores = (1 - core, core)

    def y_at(i):
        return lax.rem(y + lax.rem(lax.shift_right_logical(jnp.int32(y_digits), 2 * i), 4), ny)

    columns = [lax.rem(x + step, nx) for step in x_order]

    def send(src, dst, row, col, send_sem, recv_sem):
        pltpu.make_async_remote_copy(
            src_ref=src, dst_ref=dst, send_sem=send_sem, recv_sem=recv_sem,
            device_id=(row, z * nx + col), device_id_type=MESH,
        ).start()

    bar = pltpu.get_barrier_semaphore()

    def greet(device):
        pl.semaphore_signal(bar, inc=1, device_id=device, device_id_type=MESH)

    @pl.when(s != z)
    def _():
        greet((z, s * nx + x))

    for step in (1, nz - 1):
        greet((s, lax.rem(z + step, nz) * nx + x))

    def hops(step):
        return min(step[0], ny - step[0]) + min(step[2], nx - step[2])

    steps = [(a, b, c) for a in range(ny) for b in range(2) for c in range(nx)][1:]
    for a, b, c in sorted(steps, key=lambda step: -hops(step)):
        greet((lax.rem(y + a, ny) * 2 + lax.rem(core + b, 2), z * nx + lax.rem(x + c, nx)))

    def clear(ref):
        ref[...] = jnp.zeros(ref.shape, ref.dtype)

    @pl.when(s == 0)
    def _():
        clear(leaves.at[0])

    @pl.when(s == ns - 1)
    def _():
        clear(leaves.at[3])

    @pl.when(d == 0)
    def _():
        clear(leaves.at[1:3, 0])

    @pl.when(d == nd - 1)
    def _():
        clear(leaves.at[1:3, 3])

    clear(trs)
    for k in range(16):
        trs[2 * k : 2 * k + 2, 0:nq] = tr_ref[k]
    loads[0].wait()
    loads[2].start()
    loads[3].start()
    for i in range(2):
        for j in range(2):
            live = live_ref[i, j].astype(f32)
            for c in range(2):
                leaves[1 + i, 1 + j, c] = (raw[c, i, j].astype(f32) * live).astype(bf16)

    loads[1].wait()
    rows = min(256, total_dirs)
    for rc in range(2):
        cols = slice(rc * LANES, (rc + 1) * LANES)

        @pl.loop(0, total_dirs // rows)
        def _(n, rc=rc, cols=cols):
            right = stacked(
                *[
                    jnp.concatenate([leaves[1 + i, 1 + j, c, :, cols] for i in range(2) for j in range(2)], axis=0)
                    for c in range(2)
                ]
            )
            some = pl.ds(pl.multiple_of(n * rows, rows), rows)
            left = jnp.concatenate(
                [agg[c, i, j, some] for c in range(2) for i in range(2) for j in range(2)], axis=1
            )
            both = dot(left, right)
            for c in range(2):
                pat[rc, pl.ds(n * (rows // nq), rows // nq), c] = (
                    both[:, c * LANES : (c + 1) * LANES].astype(bf16).reshape(rows // nq, nq, LANES)
                )

    pl.semaphore_wait(bar, owners - 1 + 2 + jnp.where(s != z, 1, 0))

    def remote(src, dst, sems, i, device):
        return pltpu.make_async_remote_copy(
            src_ref=src, dst_ref=dst, send_sem=sems.at[0, i], recv_sem=sems.at[1, i],
            device_id=device, device_id_type=MESH,
        )

    swap = remote(trs, trd, t_sem, 0, (z, s * nx + x))

    left_end, right_end = x == 0, x == nx - 1
    before, after = z > 0, z < nz - 1
    left = (s, z * nx + jnp.where(left_end, nx - 1, x - 1))
    right = (s, z * nx + jnp.where(right_end, 0, x + 1))
    prev, nxt = (s, d - nx), (s, d + nx)

    def to_left(r, src=None):
        return remote(leaves.at[1 + r, 1] if src is None else src, leaves.at[1 + r, 3], nx_sem, r, left)

    def to_right(r, src=None):
        return remote(leaves.at[1 + r, 2] if src is None else src, leaves.at[1 + r, 0], nx_sem, 2 + r, right)

    first_left = remote(leaves.at[1, 1], hop.at[0], hop_sem, 0, prev)
    first_right = remote(leaves.at[1, 2], hop.at[0], hop_sem, 0, nxt)
    second_left = remote(leaves.at[2, 1], hop.at[1], hop_sem, 1, left)
    second_right = remote(leaves.at[2, 2], hop.at[1], hop_sem, 1, right)

    def pass_on(column, recv, device):
        return pltpu.make_async_remote_copy(
            src_ref=hop.at[1], dst_ref=leaves.at[2, column], send_sem=hop_sem.at[0, 2], recv_sem=nx_sem.at[1, recv],
            device_id=device, device_id_type=MESH,
        )


    spans = ((1, 3), (0, 1), (3, 4))
    up = [
        remote(leaves.at[1, a:b], leaves.at[3, a:b], ny_sem, i, (s - 1, d)) for i, (a, b) in enumerate(spans)
    ]
    down = [
        remote(leaves.at[2, a:b], leaves.at[0, a:b], ny_sem, 3 + i, (s + 1, d)) for i, (a, b) in enumerate(spans)
    ]

    def start_columns():
        for r in range(2):

            @pl.when(jnp.logical_not(left_end))
            def _(r=r):
                to_left(r).start()

            @pl.when(jnp.logical_not(right_end))
            def _(r=r):
                to_right(r).start()

        @pl.when(left_end & before)
        def _():
            second_left.start()

        @pl.when(right_end & after)
        def _():
            second_right.start()

    def start_hops():
        @pl.when(left_end & before)
        def _():
            first_left.start()

        @pl.when(right_end & after)
        def _():
            first_right.start()

    def pass_first():
        @pl.when(left_end & after)
        def _():
            first_left.wait_recv()
            to_left(0, hop.at[0]).start()

        @pl.when(right_end & before)
        def _():
            first_right.wait_recv()
            to_right(0, hop.at[0]).start()

    def pass_second():
        @pl.when(right_end & before)
        def _():
            second_left.wait_recv()
            pass_on(3, 1, prev).start()

        @pl.when(left_end & after)
        def _():
            second_right.wait_recv()
            pass_on(0, 3, nxt).start()

    def columns_came(r):
        @pl.when(d < nd - 1)
        def _():
            to_left(r).wait_recv()

        @pl.when(d > 0)
        def _():
            to_right(r).wait_recv()

    def start_up(which):
        @pl.when(s > 0)
        def _():
            for i in which:
                up[i].start()

    def start_down(which):
        @pl.when(s < ns - 1)
        def _():
            for i in which:
                down[i].start()

    start_hops()

    @pl.loop(0, 2)
    def _(rc):
        dst, arrived = grid.at[rc, 2 + s, 2 + x], r1_sem.at[rc, x // 2, y]
        for y_step in y_order:
            for other in range(2):
                row = 2 * lax.rem(y + y_step, ny) + other
                for x_step, col in zip(x_order, columns):
                    if y_step or x_step:
                        send(pat.at[rc, row * nx + col], dst, row, col, s1_sem.at[rc], arrived)
                        continue

                    @pl.when(core != other)
                    def _(row=row, col=col):
                        send(pat.at[rc, row * nx + col], dst, row, col, s1_sem.at[rc], arrived)

        pltpu.make_async_copy(pat.at[rc, me], dst, arrived).start()

    @pl.when(s != z)
    def _():
        swap.start()

    @pl.when(s == z)
    def _():
        trd[...] = trs[...]

    start_up((0,))
    start_down((0,))
    start_columns()
    for rc in range(2):
        clear(grid.at[rc, 0:2])
        clear(grid.at[rc, ns + 2 : ns + 4])

    @pl.when(z == 0)
    def _():
        for rc in range(2):
            clear(grid.at[rc, 2 : ns + 2, 0:2])

    @pl.when(z == nz - 1)
    def _():
        for rc in range(2):
            clear(grid.at[rc, 2 : ns + 2, nx + 2 : nx + 4])

    def near(p, q):
        targets = [(i, j) for i in range(2) for j in range(2) if 0 <= p - i <= 2 and 0 <= q - j <= 2]
        right = stacked(leaves[p, q, 0], leaves[p, q, 1])
        left = jnp.concatenate(
            [
                jnp.concatenate([nb[c, i, j, 3 * (p - i) + q - j] for c in range(2)], axis=1)
                for i, j in targets
            ],
            axis=0,
        )
        both = dot(left, right)
        rows = left.shape[0] // len(targets)
        width = both.shape[1] // 2
        for n, (i, j) in enumerate(targets):
            for c in range(2):
                part = both[n * rows : (n + 1) * rows, c * width : (c + 1) * width]
                part = part * live_ref[i, j].astype(f32)
                acc[c, i, j] = part if (p, q) == (1, 1) else acc[c, i, j] + part

    loads[2].wait()

    for p in range(1, 3):
        for q in range(1, 3):
            near(p, q)

    def plane(rc, side, first, count):
        rows = pl.ds(2 + first, count)
        own = grid.at[rc, rows, 2:4] if side == 0 else grid.at[rc, rows, nx : nx + 2]
        there = grid.at[rc, rows, nx + 2 : nx + 4] if side == 0 else grid.at[rc, rows, 0:2]
        return pltpu.make_async_remote_copy(
            src_ref=own, dst_ref=there, send_sem=sz_sem.at[rc, side], recv_sem=rz_sem.at[rc, side],
            device_id=(s, d - nx if side == 0 else d + nx), device_id_type=MESH,
        )

    for rc in range(2):
        @pl.loop(0, ny)
        def _(i, rc=rc):
            from_y = y_at(i)
            for side in range(2):
                part = grid.at[rc, pl.ds(2 + 2 * from_y, 2), 2 + 2 * side : 4 + 2 * side]
                pltpu.make_async_copy(part, part, r1_sem.at[rc, side, from_y]).wait()

                @pl.when(z > 0 if side == 0 else z < nz - 1)
                def _(rc=rc, side=side, from_y=from_y):
                    plane(rc, side, 2 * from_y, 2).start()

        if rc == 0:
            pass_first()
            @pl.when(s != z)
            def _():
                swap.wait_recv()

            turned = trd[...].T
            half, wide = mix.shape[1] // 2, mix.shape[2]
            lane = lax.broadcasted_iota(jnp.int32, (nq, wide), 1)
            same = lax.rem(lane, nq) == lax.broadcasted_iota(jnp.int32, (nq, wide), 0)
            imag = lax.rem(lane // nq, 2) == 1
            source = jnp.where(same, lane // (2 * nq), -1)
            for row_step in range(-2, 3):
                ks = [(k, b) for k, (a, b) in enumerate(far_offsets) if a == row_step]
                for c in range(2):
                    rows = [jnp.zeros((nq, wide), f32) for _ in range(nx)]
                    for k, b in ks:
                        p, q = (jnp.broadcast_to(turned[0:nq, 2 * k + n : 2 * k + n + 1], (nq, wide)) for n in range(2))
                        value = jnp.where(imag, p, q) if c else jnp.where(imag, -q, p)
                        rows = [jnp.where(source == 2 + col + b, value, rows[col]) for col in range(nx)]
                    for col in range(nx):
                        first = (2 * col + c) * nq
                        high = rows[col].astype(bf16)
                        mix[row_step + 2, first : first + nq] = high
                        rest = (rows[col] - high.astype(f32)).astype(bf16)
                        mix[row_step + 2, half + first : half + first + nq] = rest

    for rc in range(2):

        @pl.when(z < nz - 1)
        def _(rc=rc):
            plane(rc, 0, 0, ns).wait_recv()

        @pl.when(z > 0)
        def _(rc=rc):
            plane(rc, 1, 0, ns).wait_recv()

        @pl.loop(0, ny)
        def _(i, rc=rc):
            first = 2 * y_at(i)
            total = jnp.zeros((2 * nx * nq, 2 * LANES), f32)
            for row_step in range(5):
                right = jnp.concatenate(
                    [grid[rc, first + n + row_step].reshape(2 * (nx + 4) * nq, LANES) for n in range(2)], axis=1
                )
                term = dot(mix[row_step], right)
                total += (term[: 2 * nx * nq] + term[2 * nx * nq :]).astype(bf16).astype(f32)
            for n in range(2):
                inc[rc, pl.ds((first + n) * nx, nx)] = (
                    total[:, n * LANES : (n + 1) * LANES].astype(bf16).reshape(nx, 2, nq, LANES)
                )
            dst = back.at[rc, me]
            for n, other in enumerate(cores):
                row = first + other
                for x_step, col in zip(x_order, columns):
                    src, sems = inc.at[rc, row * nx + col], (s2_sem.at[rc], r2_sem.at[rc])
                    if n == 0 or x_step:
                        send(src, dst, row, col, *sems)
                        continue

                    @pl.when(i < ny - 1)
                    def _(src=src, row=row, col=col, sems=sems):
                        send(src, dst, row, col, *sems)

                    @pl.when(i == ny - 1)
                    def _(src=src, sems=sems):
                        pltpu.make_async_copy(src, dst, sems[1]).start()

        if rc == 0:
            pass_second()
            columns_came(0)
            start_up((1, 2))
        else:
            columns_came(1)
            start_down((1, 2))

    for p in range(1, 3):
        for q in (0, 3):
            near(p, q)

    loads[3].wait()

    def far(rc):
        cols = slice(rc * LANES, (rc + 1) * LANES)
        whole = back.at[rc]
        pltpu.make_async_copy(whole, whole, r2_sem.at[rc]).wait()
        right = stacked(*[back[rc, :, c].reshape(owners * nq, LANES) for c in range(2)])
        for i in range(2):
            left = jnp.concatenate(
                [jnp.concatenate([dis[c, i, j] for c in range(2)], axis=1) for j in range(2)], axis=0
            )
            both = dot(left, right)
            rows = left.shape[0] // 2
            for j in range(2):
                live = live_ref[i, j].astype(f32)
                for c in range(2):
                    part = both[j * rows : (j + 1) * rows, c * LANES : (c + 1) * LANES]
                    acc[c, i, j, :, cols] += part * live

    far(0)

    @pl.when(s < ns - 1)
    def _():
        for copy in up:
            copy.wait_recv()

    for q in range(4):
        near(3, q)

    @pl.when(s > 0)
    def _():
        for copy in down:
            copy.wait_recv()

    for q in range(4):
        near(0, q)

    far(1)

    @pl.when(s != z)
    def _():
        swap.wait_send()

    @pl.when(jnp.logical_not(left_end) | after)
    def _():
        to_left(0).wait_send()

    @pl.when(jnp.logical_not(right_end) | before)
    def _():
        to_right(0).wait_send()

    @pl.when(jnp.logical_not(left_end))
    def _():
        to_left(1).wait_send()

    @pl.when(jnp.logical_not(right_end))
    def _():
        to_right(1).wait_send()

    @pl.when(left_end & before | right_end & after)
    def _():
        first_left.wait_send()
        second_left.wait_send()

    @pl.when(right_end & before | left_end & after)
    def _():
        pass_on(3, 1, prev).wait_send()

    @pl.when(s > 0)
    def _():
        for copy in up:
            copy.wait_send()

    @pl.when(s < ns - 1)
    def _():
        for copy in down:
            copy.wait_send()

    for rc in range(2):
        sent = inc.at[rc, 0 : owners - 1]
        pltpu.make_async_copy(sent, sent, s1_sem.at[rc]).wait()
        pltpu.make_async_copy(sent, sent, s2_sem.at[rc]).wait()

        @pl.when(z > 0)
        def _(rc=rc):
            plane(rc, 0, 0, ns).wait_send()

        @pl.when(z < nz - 1)
        def _(rc=rc):
            plane(rc, 1, 0, ns).wait_send()


def shards(ns, nd, unknowns, leaf_live, near_blocks, aggregate, disaggregate, translate):
    nq = translate.shape[2]
    leaf, sides = unknowns.shape[3:]
    dirs = aggregate.shape[3]
    bf16, f32 = jnp.bfloat16, jnp.float32
    owners = ns * PLANE_COLS
    any_space = pl.BlockSpec(memory_space=pl.ANY)
    dma = pltpu.SemaphoreType.DMA
    field = pl.pallas_call(
        functools.partial(kernel, ns, nd),
        out_shape=pltpu.VMEM(unknowns.shape, f32),
        in_specs=[
            pl.BlockSpec(memory_space=pltpu.SMEM),
            any_space,
            any_space,
            any_space,
            any_space,
            pl.BlockSpec(memory_space=pltpu.VMEM),
        ],
        out_specs=pl.BlockSpec(memory_space=pltpu.VMEM),
        scratch_shapes=[
            pltpu.VMEM(unknowns.shape, bf16),
            pltpu.VMEM((4, 4, 2, leaf, sides), bf16),
            pltpu.VMEM((2, 2, leaf, sides), bf16),
            pltpu.VMEM(near_blocks.shape, bf16),
            pltpu.VMEM(aggregate.shape, bf16),
            pltpu.VMEM(disaggregate.shape, bf16),
            pltpu.VMEM((2, owners, 2, nq, LANES), bf16),
            pltpu.VMEM((2, ns + 4, PLANE_COLS + 4, 2, nq, LANES), bf16),
            pltpu.VMEM((2, owners, 2, nq, LANES), bf16),
            pltpu.VMEM((2, owners, 2, nq, LANES), bf16),
            pltpu.VMEM((32, LANES), f32),
            pltpu.VMEM((32, LANES), f32),
            pltpu.VMEM((5, 4 * PLANE_COLS * nq, 2 * (PLANE_COLS + 4) * nq), bf16),
            dma((4,)),
            dma((2, 3)),
            dma((2, 4)),
            dma((2, 6)),
            dma((2, 1)),
            dma((2,)),
            dma((2, 2, ns // 2)),
            dma((2, 2)),
            dma((2, 2)),
            dma((2,)),
            dma((2,)),
        ],
        compiler_params=pltpu.CompilerParams(
            collective_id=0, has_side_effects=True, vmem_limit_bytes=56 * 1024 * 1024
        ),
    )(leaf_live, unknowns, near_blocks, aggregate, disaggregate, translate)
    return field


def solution(mesh):
    in_specs = (
        P(None, "sect", "dir", None, None),
        P("sect", "dir"),
        P(None, "sect", "dir", None, None, None),
        P(None, "sect", "dir", None, None),
        P(None, "sect", "dir", None, None),
        P(None, None, "dir"),
    )
    out_specs = P(None, "sect", "dir", None, None)
    body = functools.partial(shards, mesh.shape["sect"], mesh.shape["dir"])
    return jax.shard_map(body, mesh=mesh, in_specs=in_specs, out_specs=out_specs, check_vma=False)
```
